512 devices in a mesh: src: 16 (over z_lo, core), tgt: 32 (over z_hi, y, x).
Axes of the slice: x: 4, y: 4, z: 16 (z_hi: 2, z_lo: 8; z = z_hi * 8 + z_lo), core: 2. Of those that a mesh axis runs over, the one named last changes fastest.
Arguments:
- src_feats: bfloat16 [32, 40960], P(None, ('src', 'tgt')), may hold values from -7 to 7
- src_factor: bfloat16 [16, 40960], P(None, ('src', 'tgt')), may hold values from 0.1 to 8
- tgt_feats: bfloat16 [32, 65536], P(None, ('tgt', 'src')), may hold values from -7 to 7
- tgt_factor: bfloat16 [16, 65536], P(None, ('tgt', 'src')), may hold values from 0.1 to 8
- rank_weight: float32 [16], replicated, may hold values from 0.5 to 4
Outputs:
- grad_src_feats: float32 [32, 40960], P(None, ('src', 'tgt'))
- grad_src_factor: float32 [16, 40960], P(None, ('src', 'tgt'))
- grad_tgt_feats: float32 [32, 65536], P(None, ('tgt', 'src'))
- grad_tgt_factor: float32 [16, 65536], P(None, ('tgt', 'src'))
The draws below stay inside these ranges and needn't reach their ends.
All inputs are finite; a program needn't handle non-finite values.
Results may differ from the reference program's by a relative error of at most 0.0015.
Values may be sent and summed in bfloat16 or wider, within the bound.
No kernel may reach another device: no remote copies, remote signals or barrier semaphores. Data moves between devices by JAX's collectives and lax.ppermute only.
A program may use at most 64 MiB of HBM per device.

```python
import math
import jax
import jax.numpy as jnp
from jax import lax

F = 32
RANK = 16
TGT_DEV = 128
N = 40960
M = 65536
N_SRC = 16


coarse_total = 8


fine_total = 256


heavy_factor = 8.0


def scan_points(key, point_count, salt_value):
    coarse_key = jax.random.fold_in(key, 101)
    detail_key = jax.random.fold_in(key, 202)
    coarse = jax.random.uniform(coarse_key, (coarse_total, F), jnp.float32, -4.0, 4.0)
    offsets = jax.random.uniform(detail_key, (fine_total, F), jnp.float32, -1.4, 1.4)
    parent = jnp.arange(fine_total, dtype=jnp.int32) // (fine_total // coarse_total)
    centres = coarse[parent] + offsets
    point_key = jax.random.fold_in(key, salt_value)
    assign = jax.random.randint(jax.random.fold_in(point_key, 1), (point_count,), 0, fine_total)
    log_scale = jax.random.uniform(jax.random.fold_in(point_key, 2), (point_count, 1), jnp.float32, jnp.log(0.1), jnp.log(0.8))
    jitter = jax.random.uniform(jax.random.fold_in(point_key, 3), (point_count, F), jnp.float32, -1.0, 1.0)
    jitter = jitter * (1.7320508 * jnp.exp(log_scale))
    points = centres[assign] + jitter
    return jnp.transpose(points).astype(jnp.bfloat16)


def draw_src_feats(key, part):
    return scan_points(key, N, 11)


def draw_tgt_feats(key, part):
    return scan_points(key, M, 12)


def base_factor(key, point_count):
    return jnp.exp(jax.random.uniform(key, (RANK, point_count), jnp.float32, jnp.log(0.1), jnp.log(1.0)))


def draw_src_factor(key, part):
    base = base_factor(jax.random.fold_in(key, 301), N)
    chosen = jax.random.randint(jax.random.fold_in(key, 302), (N,), 0, RANK)
    rows = jnp.arange(RANK, dtype=jnp.int32)[:, None]
    boost = jnp.where(rows == chosen[None, :], heavy_factor, 1.0)
    return (base * boost).astype(jnp.bfloat16)


def draw_tgt_factor(key, part):
    base = base_factor(jax.random.fold_in(key, 401), M)
    column = jnp.arange(M, dtype=jnp.int32)
    tgt_index = column // TGT_DEV // N_SRC
    rows = jnp.arange(RANK, dtype=jnp.int32)[:, None]
    boost = jnp.where(rows == (tgt_index % RANK)[None, :], heavy_factor, 1.0)
    return (base * boost).astype(jnp.bfloat16)


def setup_inputs(seed: int = 0) -> dict:
    splits = jax.random.split(jax.random.key(seed), 6)
    src_feats = draw_src_feats(jax.random.fold_in(splits[5], 71), 0)
    src_factor = draw_src_factor(jax.random.fold_in(splits[5], 71), 0)
    tgt_feats = draw_tgt_feats(jax.random.fold_in(splits[5], 71), 0)
    tgt_factor = draw_tgt_factor(jax.random.fold_in(splits[5], 71), 0)
    rank_weight = jnp.clip(jnp.exp(jax.random.uniform(splits[4], (RANK,), jnp.float32, math.log(0.5), math.log(4.0))), 0.5, 4.0)
    return dict(src_feats=src_feats, src_factor=src_factor, tgt_feats=tgt_feats, tgt_factor=tgt_factor, rank_weight=rank_weight)


def tile_terms(src_x, src_q, tgt_y, scaled_r, inverse_g):
    sq_src = lax.optimization_barrier(jnp.sum(jnp.square(src_x.astype(jnp.float32)), 0))
    sq_tgt = lax.optimization_barrier(jnp.sum(jnp.square(tgt_y.astype(jnp.float32)), 0))
    inner_prod = jnp.dot(src_x.T, tgt_y, preferred_element_type=jnp.float32)
    distance = jnp.sqrt(sq_src[:, None] + sq_tgt[None, :] - 2.0 * inner_prod + 1.0)
    plan_tile = jnp.dot(src_q.T, scaled_r, preferred_element_type=jnp.float32)
    weight = (plan_tile / distance).astype(jnp.bfloat16)
    cost_bf = distance.astype(jnp.bfloat16)
    row_mass = lax.optimization_barrier(jnp.sum(weight.astype(jnp.float32), 1))
    col_mass = lax.optimization_barrier(jnp.sum(weight.astype(jnp.float32), 0))
    grad_x = src_x.astype(jnp.float32) * row_mass[None, :] - jnp.dot(tgt_y, weight.T, preferred_element_type=jnp.float32)
    grad_q = jnp.dot(scaled_r, cost_bf.T, preferred_element_type=jnp.float32)
    grad_y = tgt_y.astype(jnp.float32) * col_mass[None, :] - jnp.dot(src_x, weight, preferred_element_type=jnp.float32)
    grad_r = inverse_g[:, None] * jnp.dot(src_q, cost_bf, preferred_element_type=jnp.float32)
    return (jnp.concatenate([grad_x, grad_q], 0), jnp.concatenate([grad_y, grad_r], 0))

def reference(src_feats, src_factor, tgt_feats, tgt_factor, rank_weight):
    inverse_g = 1.0 / rank_weight
    scaled_r = (tgt_factor.astype(jnp.float32) * inverse_g[:, None]).astype(jnp.bfloat16)
    feature_count = src_feats.shape[0]
    total_src = src_feats.shape[1]
    total_tgt = tgt_feats.shape[1]
    block_rows = 512 if total_src % 512 == 0 else total_src
    block_count = total_src // block_rows

    def advance(totals, block_index):
        offset = (block_index * block_rows).astype(jnp.int32)
        src_x = lax.dynamic_slice_in_dim(src_feats, offset, block_rows, 1)
        src_q = lax.dynamic_slice_in_dim(src_factor, offset, block_rows, 1)
        src_part, tgt_part = tile_terms(src_x, src_q, tgt_feats, scaled_r, inverse_g)
        return (totals + tgt_part, src_part)
    start_totals = jnp.zeros((feature_count + src_factor.shape[0], total_tgt), jnp.float32)
    tgt_sum, src_blocks = lax.scan(advance, start_totals, jnp.arange(block_count, dtype=jnp.int32))
    src_sum = jnp.transpose(src_blocks, (1, 0, 2)).reshape(feature_count + src_factor.shape[0], total_src)
    scale = 1.0 / total_tgt
    return (src_sum[:feature_count] * scale, src_sum[feature_count:] * scale, tgt_sum[:feature_count] * scale, tgt_sum[feature_count:] * scale)
```

```python
import jax
import jax.numpy as jnp
from jax import lax
from jax.sharding import Mesh
from jax.sharding import PartitionSpec as P

RING = ("zh", "zl")
PLANE = ("y", "x", "core")


def tile_terms(src_x, src_q, tgt_y, scaled_r, inverse_g):
    sq_src = jnp.sum(jnp.square(src_x.astype(jnp.float32)), 0)
    sq_tgt = jnp.sum(jnp.square(tgt_y.astype(jnp.float32)), 0)
    inner_prod = jnp.dot(src_x.T, tgt_y, preferred_element_type=jnp.float32)
    distance = jnp.sqrt(sq_src[:, None] + sq_tgt[None, :] - 2.0 * inner_prod + 1.0)
    plan_tile = jnp.dot(src_q.T, scaled_r, preferred_element_type=jnp.float32)
    weight = (plan_tile / distance).astype(jnp.bfloat16)
    cost_bf = distance.astype(jnp.bfloat16)
    row_mass = jnp.sum(weight.astype(jnp.float32), 1)
    col_mass = jnp.sum(weight.astype(jnp.float32), 0)
    grad_x = src_x.astype(jnp.float32) * row_mass[None, :] - jnp.dot(
        tgt_y, weight.T, preferred_element_type=jnp.float32
    )
    grad_q = jnp.dot(scaled_r, cost_bf.T, preferred_element_type=jnp.float32)
    grad_y = tgt_y.astype(jnp.float32) * col_mass[None, :] - jnp.dot(
        src_x, weight, preferred_element_type=jnp.float32
    )
    grad_r = inverse_g[:, None] * jnp.dot(src_q, cost_bf, preferred_element_type=jnp.float32)
    return (jnp.concatenate([grad_x, grad_q], 0), jnp.concatenate([grad_y, grad_r], 0))


def gather_blocks(block, axes):
    count = lax.axis_size(axes)
    copies = jnp.broadcast_to(block[None], (count, *block.shape))
    return lax.all_to_all(copies, axes, 0, 0, tiled=True)


def join(blocks):
    count, rows, cols = blocks.shape
    return jnp.transpose(blocks, (1, 0, 2)).reshape(rows, count * cols)


def reduce_blocks(whole, axes):
    count = lax.axis_size(axes)
    rows, cols = whole.shape
    parts = jnp.transpose(whole.reshape(rows, count, cols // count), (1, 0, 2))
    return jnp.sum(lax.all_to_all(parts, axes, 0, 0, tiled=True), 0)


def local(src_feats, src_factor, tgt_feats, tgt_factor, rank_weight):
    features = src_feats.shape[0]
    inverse_g = 1.0 / rank_weight
    total_tgt = tgt_feats.shape[1] * lax.axis_size(RING) * lax.axis_size(PLANE)
    src_whole = join(gather_blocks(jnp.concatenate([src_feats, src_factor], 0), PLANE))
    tgt_whole = join(gather_blocks(jnp.concatenate([tgt_feats, tgt_factor], 0), RING))
    tgt_points = tgt_whole[:features]
    scaled_r = (tgt_whole[features:].astype(jnp.float32) * inverse_g[:, None]).astype(
        jnp.bfloat16
    )
    rows = src_whole.shape[0]
    row_count = src_whole.shape[1]
    col_count = tgt_points.shape[1]
    block_rows = 512

    def advance(block_index, totals):
        src_acc, tgt_acc = totals
        offset = block_index * block_rows
        part = lax.dynamic_slice_in_dim(src_whole, offset, block_rows, 1)
        src_part, tgt_part = tile_terms(
            part[:features], part[features:], tgt_points, scaled_r, inverse_g
        )
        src_acc = lax.dynamic_update_slice_in_dim(src_acc, src_part, offset, 1)
        return (src_acc, tgt_acc + tgt_part)

    src_start = jnp.zeros((rows, row_count), jnp.float32)
    tgt_start = jnp.zeros((rows, col_count), jnp.float32)
    src_terms, tgt_terms = lax.fori_loop(
        0, row_count // block_rows, advance, (src_start, tgt_start)
    )
    tgt_sum = reduce_blocks(tgt_terms, RING)
    src_sum = reduce_blocks(src_terms, PLANE)
    scale = 1.0 / total_tgt
    return (
        src_sum[:features] * scale,
        src_sum[features:] * scale,
        tgt_sum[:features] * scale,
        tgt_sum[features:] * scale,
    )


def solution(mesh):
    fine = Mesh(mesh.devices.reshape(8, 2, 2, 4, 4), ("zl", "core", "zh", "y", "x"))
    src_axes = ("zl", "core", "zh", "y", "x")
    tgt_axes = ("zh", "y", "x", "zl", "core")
    by_src = P(None, src_axes)
    by_tgt = P(None, tgt_axes)
    return jax.shard_map(
        local,
        mesh=fine,
        in_specs=(by_src, by_src, by_tgt, by_tgt, P()),
        out_specs=(by_src, by_src, by_tgt, by_tgt),
        check_vma=False,
    )
```

```python
import jax
import jax.numpy as jnp
from jax import lax
from jax.experimental import pallas as pl
from jax.experimental.pallas import tpu as pltpu
from jax.sharding import Mesh
from jax.sharding import PartitionSpec as P

RING = ("zh", "zl")
PLANE = ("y", "x", "core")
BF16 = jnp.bfloat16
F32 = jnp.float32
VMEM = pl.BlockSpec(memory_space=pltpu.VMEM)
SMEM = pl.BlockSpec(memory_space=pltpu.SMEM)
STEP = 256


def dot(a, b):
    return jnp.dot(a, b, preferred_element_type=F32)


def inverse_column(rank_ref, width):
    rank = rank_ref.shape[0]
    rows = lax.broadcasted_iota(jnp.int32, (rank, width), 0)
    column = jnp.full((rank, width), rank_ref[0], F32)
    for k in range(1, rank):
        column = jnp.where(rows == k, rank_ref[k], column)
    return 1.0 / column


def copies_kernel(feats_ref, factor_ref, out_ref):
    block = jnp.concatenate([feats_ref[...], factor_ref[...]], 0)
    for member in range(out_ref.shape[0]):
        out_ref[member] = block


def scaled_copies_kernel(rank_ref, feats_ref, factor_ref, out_ref):
    factor = factor_ref[...]
    inverse_g = inverse_column(rank_ref, factor.shape[1])
    scaled = (factor.astype(F32) * inverse_g).astype(BF16)
    block = jnp.concatenate([feats_ref[...], scaled], 0)
    for member in range(out_ref.shape[0]):
        out_ref[member] = block


def three_parts(value):
    high = value.astype(BF16)
    rest = value - high.astype(F32)
    mid = rest.astype(BF16)
    low = (rest - mid.astype(F32)).astype(BF16)
    return [high.astype(F32), mid.astype(F32), low.astype(F32)]


def squares(feats):
    return jnp.sum(jnp.square(feats), 0, keepdims=True)


def pair_kernel(features, scale, is_target, rank_ref, lane_ref, sub_ref, out_ref, a_ref, gw_ref, gc_ref, bd_ref, bp_ref, x_ref, sum_ref):
    lane_blocks, rows, lane_width = lane_ref.shape
    sub_blocks, _, sub_width = sub_ref.shape
    rank = rows - features
    for b in range(sub_blocks):
        block = sub_ref[b].astype(F32)
        x = block[:features]
        q = block[features:]
        ones = jnp.ones((1, sub_width), F32)
        stack = jnp.concatenate(
            [-2.0 * x, q] + three_parts(squares(x)) + [ones] * 3 + [jnp.zeros((10, sub_width), F32)], 0
        )
        at = pl.ds(b * sub_width, sub_width)
        a_ref[at, :] = stack.T.astype(BF16)
        gw_ref[:, at] = jnp.concatenate([x, ones, jnp.zeros((7, sub_width), F32)], 0)
        gc_ref[:, at] = q
    for b in range(lane_blocks):
        x_ref[:, pl.ds(b * lane_width, lane_width)] = lane_ref[b].astype(F32)
    lanes = x_ref.shape[1]
    subs = a_ref.shape[0]
    for start in range(0, lanes, STEP):
        at = pl.ds(start, STEP)
        block = x_ref[:, at]
        x = block[:features]
        ones = jnp.ones((3, STEP), F32)
        tail = jnp.zeros((10, STEP), F32)
        bd_ref[:, at] = jnp.concatenate(
            [x, jnp.zeros((rank, STEP), F32), ones] + three_parts(squares(x) + 1.0) + [tail], 0
        ).astype(BF16)
        bp_ref[:, at] = jnp.concatenate(
            [jnp.zeros((features, STEP), F32), block[features:], jnp.zeros((16, STEP), F32)], 0
        ).astype(BF16)
    gw = gw_ref[...].astype(BF16)
    gc = gc_ref[...].astype(BF16)
    if is_target:
        factor_scale = inverse_column(rank_ref, STEP) * scale
    else:
        factor_scale = scale

    def advance(index, carry):
        at = pl.ds(pl.multiple_of(index * STEP, STEP), STEP)
        bd = bd_ref[:, at]
        bp = bp_ref[:, at]
        sum_w = jnp.zeros((gw.shape[0], STEP), F32)
        sum_c = jnp.zeros((rank, STEP), F32)
        for u in range(0, subs, STEP):
            a = a_ref[pl.ds(u, STEP), :]
            s = dot(a, bd)
            p = dot(a, bp)
            r = lax.rsqrt(s)
            w = (p * r).astype(BF16)
            c = (s * r).astype(BF16)
            sum_w += dot(gw[:, u : u + STEP], w)
            sum_c += dot(gc[:, u : u + STEP], c)
        x = x_ref[:, at][:features]
        grad = (x * sum_w[features : features + 1] - sum_w[:features]) * scale
        both = jnp.concatenate([grad, sum_c * factor_scale], 0)
        if is_target:
            per = STEP // lane_width
            for k in range(per):
                out_ref[index * per + k] = both[:, k * lane_width : (k + 1) * lane_width]
        else:
            sum_ref[:, at] = both
        return carry

    lax.fori_loop(0, lanes // STEP, advance, 0)
    if not is_target:
        half = lane_width // 2
        for b in range(lane_blocks):
            block = sum_ref[:, b * lane_width : (b + 1) * lane_width]
            factor = block[features:]
            out_ref[b] = jnp.concatenate(
                [
                    block[:features],
                    jnp.concatenate([factor[:, :half], factor[:, half:]], 0),
                    jnp.zeros((features, 128 - lane_width - half), F32),
                ],
                1,
            )


def target_sum_kernel(features, parts_ref, feats_ref, factor_ref):
    total = jnp.sum(parts_ref[...], 0)
    feats_ref[...] = total[:features]
    factor_ref[...] = total[features:]


def source_sum_kernel(rank, parts_ref, feats_ref, factor_ref):
    total = jnp.sum(parts_ref[...], 0)
    width = feats_ref.shape[1]
    half = width // 2
    feats_ref[...] = total[:, :width]
    factor_ref[:, :half] = total[:rank, width : width + half]
    factor_ref[:, half:] = total[rank:, width : width + half]


def call(kernel, specs, outs, scratch=(), flops=0):
    single = not isinstance(outs, tuple)
    return pl.pallas_call(
        kernel,
        out_shape=outs,
        in_specs=specs,
        out_specs=VMEM if single else tuple(VMEM for _ in outs),
        scratch_shapes=scratch,
        compiler_params=pltpu.CompilerParams(vmem_limit_bytes=40 << 20),
        cost_estimate=pl.CostEstimate(flops=flops, transcendentals=0, bytes_accessed=1 << 20),
    )


def exchange(blocks, axes):
    return lax.all_to_all(blocks, axes, 0, 0, tiled=True)


def local(src_feats, src_factor, tgt_feats, tgt_factor, rank_weight):
    features, src_width = src_feats.shape
    rank = src_factor.shape[0]
    rows = features + rank
    tgt_width = tgt_feats.shape[1]
    ring = lax.axis_size(RING)
    plane = lax.axis_size(PLANE)
    scale = 1.0 / (tgt_width * ring * plane)
    sources = ring * src_width
    targets = plane * tgt_width

    def shape(*dims, dtype=F32):
        return jax.ShapeDtypeStruct(dims, dtype)

    tgt_copies = call(scaled_copies_kernel, (SMEM, VMEM, VMEM), shape(plane, rows, tgt_width, dtype=BF16))(
        rank_weight, tgt_feats, tgt_factor
    )
    src_copies = call(copies_kernel, (VMEM, VMEM), shape(ring, rows, src_width, dtype=BF16))(
        src_feats, src_factor
    )
    tgt_blocks = exchange(tgt_copies, PLANE)
    src_blocks = exchange(src_copies, RING)

    def pairs(is_target, lane_blocks, sub_blocks, out):
        lanes = lane_blocks.shape[0] * lane_blocks.shape[2]
        subs = sub_blocks.shape[0] * sub_blocks.shape[2]
        scratch = (
            pltpu.VMEM((subs, 64), BF16),
            pltpu.VMEM((features + 8, subs), F32),
            pltpu.VMEM((rank, subs), F32),
            pltpu.VMEM((64, lanes), BF16),
            pltpu.VMEM((64, lanes), BF16),
            pltpu.VMEM((rows, lanes), F32),
            pltpu.VMEM((rows, lanes), F32),
        )

        def kernel(*refs):
            pair_kernel(features, scale, is_target, *refs)

        return call(kernel, (SMEM, VMEM, VMEM), out, scratch, flops=lanes * subs * 2 * 256 * 4)(
            rank_weight, lane_blocks, sub_blocks
        )

    tgt_parts = pairs(True, tgt_blocks, src_blocks, shape(plane, rows, tgt_width))
    tgt_parts = exchange(tgt_parts, PLANE)
    src_parts = pairs(False, src_blocks, tgt_blocks, shape(ring, features, 128))
    src_parts = exchange(src_parts, RING)

    def tgt_final(*refs):
        target_sum_kernel(features, *refs)

    def src_final(*refs):
        source_sum_kernel(rank, *refs)

    grad_y, grad_r = call(tgt_final, (VMEM,), (shape(features, tgt_width), shape(rank, tgt_width)))(tgt_parts)
    grad_x, grad_q = call(src_final, (VMEM,), (shape(features, src_width), shape(rank, src_width)))(src_parts)
    return grad_x, grad_q, grad_y, grad_r


def solution(mesh):
    fine = Mesh(mesh.devices.reshape(8, 2, 2, 4, 4), ("zl", "core", "zh", "y", "x"))
    by_src = P(None, ("zl", "core", "zh", "y", "x"))
    by_tgt = P(None, ("zh", "y", "x", "zl", "core"))
    return jax.shard_map(
        local,
        mesh=fine,
        in_specs=(by_src, by_src, by_tgt, by_tgt, P()),
        out_specs=(by_src, by_src, by_tgt, by_tgt),
        check_vma=False,
    )
```

```python
import jax
import jax.numpy as jnp
from jax import lax
from jax.experimental import pallas as pl
from jax.experimental.pallas import tpu as pltpu
from jax.sharding import Mesh
from jax.sharding import PartitionSpec as P

RING = ("zh", "zl")
PLANE = ("y", "x")
CORE = "core"
BF16 = jnp.bfloat16
F32 = jnp.float32
VMEM = pl.BlockSpec(memory_space=pltpu.VMEM)
HBM = pl.BlockSpec(memory_space=pltpu.HBM)
LANES = 128


def dot(a, b):
    return jnp.dot(a, b, preferred_element_type=F32)


def inverse_column(rank_ref, width):
    rank = rank_ref.shape[0]
    rows = lax.broadcasted_iota(jnp.int32, (rank, width), 0)
    column = jnp.full((rank, width), rank_ref[0], F32)
    for k in range(1, rank):
        column = jnp.where(rows == k, rank_ref[k], column)
    return 1.0 / column


def pack(feats, factor):
    rows, width = feats.shape
    half = width // 2
    halves = jnp.concatenate([factor[:, :half], factor[:, half:]], 0)
    return jnp.concatenate([feats, halves, jnp.zeros((rows, LANES - width - half), F32)], 1)


def unpack(block, rank, width):
    half = width // 2
    halves = block[:, width : width + half]
    return block[:, :width], jnp.concatenate([halves[:rank], halves[rank:]], 1)


def source_copies_kernel(feats_ref, factor_ref, out_ref):
    block = pack(feats_ref[...].astype(F32), factor_ref[...].astype(F32)).astype(BF16)
    for member in range(out_ref.shape[0]):
        out_ref[member] = block


def target_copies_kernel(rank_hbm, feats_hbm, factor_hbm, out_ref, inverse_ref, rank_ref, feats_ref, factor_ref, sems):
    pairs = [(rank_hbm, rank_ref), (feats_hbm, feats_ref), (factor_hbm, factor_ref)]
    loads = [pltpu.make_async_copy(a, b, sems.at[k]) for k, (a, b) in enumerate(pairs)]
    for load in loads:
        load.start()
    for load in loads:
        load.wait()
    factor = factor_ref[...]
    inverse_g = inverse_column(rank_ref, factor.shape[1])
    inverse_ref[...] = inverse_g
    scaled = (factor.astype(F32) * inverse_g).astype(BF16)
    block = jnp.concatenate([feats_ref[...], scaled], 0)
    for member in range(out_ref.shape[0]):
        out_ref[member] = block


def three_parts(value):
    high = value.astype(BF16).astype(F32)
    rest = value - high
    mid = rest.astype(BF16).astype(F32)
    low = (rest - mid).astype(BF16).astype(F32)
    return [high, mid, low]


def squares(feats):
    return jnp.sum(jnp.square(feats), 0, keepdims=True)


def put_sublanes(at, x, q, a_ref, gw_ref, gc_ref):
    width = x.shape[1]
    ones = jnp.ones((1, width), F32)
    stack = jnp.concatenate(
        [-2.0 * x, q] + three_parts(squares(x)) + [ones] * 3 + [jnp.zeros((10, width), F32)], 0
    )
    a_ref[at, :] = stack.T.astype(BF16)
    gw_ref[:, at] = jnp.concatenate([x, ones, jnp.zeros((7, width), F32)], 0).astype(gw_ref.dtype)
    gc_ref[:, at] = q.astype(gc_ref.dtype)


def put_lanes(at, x, q, bd_ref, bp_ref):
    features, width = x.shape
    rank = q.shape[0]
    bd_ref[:, at] = jnp.concatenate(
        [x, jnp.zeros((rank, width), F32), jnp.ones((3, width), F32)]
        + three_parts(squares(x) + 1.0)
        + [jnp.zeros((10, width), F32)],
        0,
    ).astype(BF16)
    bp_ref[:, at] = jnp.concatenate(
        [jnp.zeros((features, width), F32), q, jnp.zeros((16, width), F32)], 0
    ).astype(BF16)


def pair_sums(a_ref, gw, gc, bd, bp, step):
    lanes = bd.shape[1]
    sum_w = jnp.zeros((gw.shape[0], lanes), F32)
    sum_c = jnp.zeros((gc.shape[0], lanes), F32)
    for u in range(0, a_ref.shape[0], step):
        a = a_ref[pl.ds(u, step), :]
        s = dot(a, bd)
        p = dot(a, bp)
        r = lax.rsqrt(s)
        sum_w += dot(gw[:, u : u + step], (p * r).astype(BF16))
        sum_c += dot(gc[:, u : u + step], (s * r).astype(BF16))
    return sum_w, sum_c


def feature_gradient(x, sum_w, scale):
    features = x.shape[0]
    return (x * sum_w[features : features + 1] - sum_w[:features]) * scale


def target_prepare_kernel(features, own_ref, other_ref, a_ref, gw_ref, gc_ref, bd_ref, bp_ref):
    count, _, width = own_ref.shape
    for b in range(2 * count):
        block = (own_ref[b] if b < count else other_ref[b - count]).astype(F32)
        at = pl.ds(b * width, width)
        put_sublanes(at, block[:features], block[features:], a_ref, gw_ref, gc_ref)
        put_lanes(at, block[:features], block[features:], bd_ref, bp_ref)


def source_pair_kernel(scale, width, src_ref, a_ref, gw_ref, gc_ref, out_ref, x_ref, q_ref, bd_ref, bp_ref, sum_ref):
    count, features, _ = src_ref.shape
    rank = gc_ref.shape[0]
    for b in range(count):
        x, q = unpack(src_ref[b].astype(F32), rank, width)
        x_ref[:, b * width : (b + 1) * width] = x
        q_ref[:, b * width : (b + 1) * width] = q
    lanes = x_ref.shape[1]
    put_lanes(slice(None), x_ref[...], q_ref[...], bd_ref, bp_ref)
    gw = gw_ref[...]
    gc = gc_ref[...]
    step = lanes // 2
    for start in range(0, lanes, step):
        at = slice(start, start + step)
        sum_w, sum_c = pair_sums(a_ref, gw, gc, bd_ref[:, at], bp_ref[:, at], 1024)
        sum_ref[:features, at] = feature_gradient(x_ref[:, at], sum_w, scale)
        sum_ref[features:, at] = sum_c * scale
    for b in range(count):
        block = sum_ref[:, b * width : (b + 1) * width]
        out_ref[b] = pack(block[:features], block[features:])


def target_pair_kernel(scale, src_width, inverse_ref, src_ref, own_ref, other_ref, bd_ref, bp_ref, keep_ref, send_ref, a_ref, gw_ref, gc_ref):
    src_count, features, _ = src_ref.shape
    rank = own_ref.shape[1] - features
    for b in range(src_count):
        x, q = unpack(src_ref[b].astype(F32), rank, src_width)
        put_sublanes(pl.ds(b * src_width, src_width), x, q, a_ref, gw_ref, gc_ref)
    gw = gw_ref[...].astype(BF16)
    gc = gc_ref[...].astype(BF16)
    count, _, width = own_ref.shape
    factor_scale = inverse_ref[...] * scale
    group = 8
    step = group * width
    for half, (from_ref, to_ref) in enumerate([(own_ref, keep_ref), (other_ref, send_ref)]):

        def advance(index, carry):
            at = pl.ds(pl.multiple_of(half * count * width + index * step, step), step)
            sum_w, sum_c = pair_sums(a_ref, gw, gc, bd_ref[:, at], bp_ref[:, at], a_ref.shape[0] // 2)
            for k in range(group):
                lanes = slice(k * width, (k + 1) * width)
                x = from_ref[index * group + k][:features].astype(F32)
                grad = feature_gradient(x, sum_w[:, lanes], scale)
                to_ref[index * group + k] = jnp.concatenate([grad, sum_c[:, lanes] * factor_scale], 0)
            return carry

        lax.fori_loop(0, count // group, advance, 0)


def target_sum_kernel(features, parts_ref, feats_ref, factor_ref):
    total = jnp.sum(parts_ref[...], 0)
    feats_ref[...] = total[:features]
    factor_ref[...] = total[features:]


def source_sum_kernel(parts_ref, feats_ref, factor_ref):
    rank, width = factor_ref.shape
    feats, factor = unpack(jnp.sum(parts_ref[...], 0), rank, width)
    feats_ref[...] = feats
    factor_ref[...] = factor


def call(kernel, specs, outs, scratch=(), flops=0):
    single = not isinstance(outs, tuple)
    return pl.pallas_call(
        kernel,
        out_shape=outs,
        in_specs=specs,
        out_specs=VMEM if single else tuple(VMEM for _ in outs),
        scratch_shapes=scratch,
        compiler_params=pltpu.CompilerParams(vmem_limit_bytes=40 << 20),
        cost_estimate=pl.CostEstimate(flops=flops, transcendentals=0, bytes_accessed=1 << 20),
    )


def shape(*dims, dtype=F32):
    return jax.ShapeDtypeStruct(dims, dtype)


def exchange(blocks, axes):
    return lax.all_to_all(blocks, axes, 0, 0, tiled=True)


def swap(blocks):
    return lax.ppermute(blocks, CORE, [(0, 1), (1, 0)])


def local(src_feats, src_factor, tgt_feats, tgt_factor, rank_weight):
    features, src_width = src_feats.shape
    rank = src_factor.shape[0]
    rows = features + rank
    tgt_width = tgt_feats.shape[1]
    ring = lax.axis_size(RING)
    plane = lax.axis_size(PLANE)
    scale = 1.0 / (tgt_width * ring * plane * lax.axis_size(CORE))
    sources = ring * src_width
    targets = 2 * plane * tgt_width

    tgt_copies, inverse_g = call(
        target_copies_kernel,
        (HBM,) * 3,
        (shape(plane, rows, tgt_width, dtype=BF16), shape(rank, tgt_width)),
        (
            pltpu.SMEM((rank,), F32),
            pltpu.VMEM((features, tgt_width), BF16),
            pltpu.VMEM((rank, tgt_width), BF16),
            pltpu.SemaphoreType.DMA((3,)),
        ),
    )(*(pltpu.with_memory_space_constraint(array, pltpu.HBM) for array in (rank_weight, tgt_feats, tgt_factor)))
    src_copies = call(source_copies_kernel, (VMEM, VMEM), shape(ring, features, LANES, dtype=BF16))(
        src_feats, src_factor
    )
    tgt_own = exchange(tgt_copies, PLANE)
    tgt_own, src_copies = lax.optimization_barrier((tgt_own, src_copies))
    src_blocks = exchange(src_copies, RING)
    tgt_other = swap(tgt_own)

    a, gw, gc, bd, bp = call(
        lambda *refs: target_prepare_kernel(features, *refs),
        (VMEM, VMEM),
        (
            shape(targets, 64, dtype=BF16),
            shape(features + 8, targets, dtype=BF16),
            shape(rank, targets, dtype=BF16),
            shape(64, targets, dtype=BF16),
            shape(64, targets, dtype=BF16),
        ),
        flops=1 << 22,
    )(tgt_own, tgt_other)

    flops = sources * targets * 2 * 256 * 4
    src_parts = call(
        lambda *refs: source_pair_kernel(scale, src_width, *refs),
        (VMEM,) * 4,
        shape(ring, features, LANES),
        (
            pltpu.VMEM((features, sources), F32),
            pltpu.VMEM((rank, sources), F32),
            pltpu.VMEM((64, sources), BF16),
            pltpu.VMEM((64, sources), BF16),
            pltpu.VMEM((rows, sources), F32),
        ),
        flops,
    )(src_blocks, a, gw, gc)
    src_sums = exchange(src_parts, RING)
    keep, send = call(
        lambda *refs: target_pair_kernel(scale, src_width, *refs),
        (VMEM,) * 6,
        (shape(plane, rows, tgt_width), shape(plane, rows, tgt_width)),
        (
            pltpu.VMEM((sources, 64), BF16),
            pltpu.VMEM((features + 8, sources), F32),
            pltpu.VMEM((rank, sources), F32),
        ),
        flops,
    )(inverse_g, src_blocks, tgt_own, tgt_other, bd, bp)
    src_sums, tgt_half = lax.optimization_barrier((src_sums, keep + swap(send)))
    tgt_sums = exchange(tgt_half, PLANE)

    grad_x, grad_q = call(source_sum_kernel, (VMEM,), (shape(features, src_width), shape(rank, src_width)))(src_sums)
    grad_y, grad_r = call(
        lambda *refs: target_sum_kernel(features, *refs), (VMEM,), (shape(features, tgt_width), shape(rank, tgt_width))
    )(tgt_sums)
    return grad_x, grad_q, grad_y, grad_r


def solution(mesh):
    fine = Mesh(mesh.devices.reshape(8, 2, 2, 4, 4), ("zl", "core", "zh", "y", "x"))
    by_src = P(None, ("zl", "core", "zh", "y", "x"))
    by_tgt = P(None, ("zh", "y", "x", "zl", "core"))
    return jax.shard_map(
        local,
        mesh=fine,
        in_specs=(by_src, by_src, by_tgt, by_tgt, P()),
        out_specs=(by_src, by_src, by_tgt, by_tgt),
        check_vma=False,
    )
```

```python
import jax
import jax.numpy as jnp
from jax import lax
from jax.experimental import pallas as pl
from jax.experimental.pallas import tpu as pltpu
from jax.sharding import Mesh
from jax.sharding import PartitionSpec as P

RING = ("zh", "zl")
PLANE = ("y", "x")
CORE = "core"
BF16 = jnp.bfloat16
F32 = jnp.float32
VMEM = pl.BlockSpec(memory_space=pltpu.VMEM)
HBM = pl.BlockSpec(memory_space=pltpu.HBM)
LANES = 128


def dot(a, b):
    return jnp.dot(a, b, preferred_element_type=F32)


def inverse_column(rank_ref, width):
    rank = rank_ref.shape[0]
    rows = lax.broadcasted_iota(jnp.int32, (rank, width), 0)
    column = jnp.full((rank, width), rank_ref[0], F32)
    for k in range(1, rank):
        column = jnp.where(rows == k, rank_ref[k], column)
    return 1.0 / column


def pack(feats, factor):
    rows, width = feats.shape
    half = width // 2
    halves = jnp.concatenate([factor[:, :half], factor[:, half:]], 0)
    return jnp.concatenate([feats, halves, jnp.zeros((rows, LANES - width - half), F32)], 1)


def unpack(block, rank, width):
    half = width // 2
    halves = block[:, width : width + half]
    return block[:, :width], jnp.concatenate([halves[:rank], halves[rank:]], 1)


def source_copies_kernel(feats_ref, factor_ref, out_ref):
    block = pack(feats_ref[...].astype(F32), factor_ref[...].astype(F32)).astype(BF16)
    for member in range(out_ref.shape[0]):
        out_ref[member] = block


def target_copies_kernel(rank_hbm, feats_hbm, factor_hbm, out_ref, inverse_ref, rank_ref, feats_ref, factor_ref, sems):
    pairs = [(rank_hbm, rank_ref), (feats_hbm, feats_ref), (factor_hbm, factor_ref)]
    loads = [pltpu.make_async_copy(a, b, sems.at[k]) for k, (a, b) in enumerate(pairs)]
    for load in loads:
        load.start()
    for load in loads:
        load.wait()
    factor = factor_ref[...]
    inverse_g = inverse_column(rank_ref, factor.shape[1])
    inverse_ref[...] = inverse_g
    scaled = (factor.astype(F32) * inverse_g).astype(BF16)
    block = jnp.concatenate([feats_ref[...], scaled], 0)
    for member in range(out_ref.shape[0]):
        out_ref[member] = block


def three_parts(value):
    high = value.astype(BF16).astype(F32)
    rest = value - high
    mid = rest.astype(BF16).astype(F32)
    low = (rest - mid).astype(BF16).astype(F32)
    return [high, mid, low]


def squares(feats):
    return jnp.sum(jnp.square(feats), 0, keepdims=True)


def put_sublanes(at, x, q, a_ref, gw_ref, gc_ref):
    width = x.shape[1]
    ones = jnp.ones((1, width), F32)
    stack = jnp.concatenate(
        [-2.0 * x, q] + three_parts(squares(x)) + [ones] * 3 + [jnp.zeros((10, width), F32)], 0
    )
    a_ref[at, :] = stack.T.astype(BF16)
    gw_ref[:, at] = jnp.concatenate([x, ones, jnp.zeros((7, width), F32)], 0).astype(gw_ref.dtype)
    gc_ref[:, at] = q.astype(gc_ref.dtype)


def put_lanes(at, x, q, bd_ref, bp_ref):
    features, width = x.shape
    rank = q.shape[0]
    bd_ref[:, at] = jnp.concatenate(
        [x, jnp.zeros((rank, width), F32), jnp.ones((3, width), F32)]
        + three_parts(squares(x) + 1.0)
        + [jnp.zeros((10, width), F32)],
        0,
    ).astype(BF16)
    bp_ref[:, at] = jnp.concatenate(
        [jnp.zeros((features, width), F32), q, jnp.zeros((16, width), F32)], 0
    ).astype(BF16)


def pair_sums(a_ref, gw, gc, bd, bp, step):
    lanes = bd.shape[1]
    sum_w = jnp.zeros((gw.shape[0], lanes), F32)
    sum_c = jnp.zeros((gc.shape[0], lanes), F32)
    for u in range(0, a_ref.shape[0], step):
        a = a_ref[pl.ds(u, step), :]
        s = dot(a, bd)
        p = dot(a, bp)
        r = lax.rsqrt(s)
        sum_w += dot(gw[:, u : u + step], (p * r).astype(BF16))
        sum_c += dot(gc[:, u : u + step], (s * r).astype(BF16))
    return sum_w, sum_c


def feature_gradient(x, sum_w, scale):
    features = x.shape[0]
    return (x * sum_w[features : features + 1] - sum_w[:features]) * scale


def target_prepare_kernel(features, own_ref, other_ref, a_ref, gw_ref, gc_ref, own_bd, own_bp, other_bd, other_bp):
    count, _, width = own_ref.shape
    for half, (ref, bd_ref, bp_ref) in enumerate([(own_ref, own_bd, own_bp), (other_ref, other_bd, other_bp)]):
        for b in range(count):
            block = ref[b].astype(F32)
            put_sublanes(
                pl.ds((half * count + b) * width, width), block[:features], block[features:], a_ref, gw_ref, gc_ref
            )
            put_lanes(pl.ds(b * width, width), block[:features], block[features:], bd_ref, bp_ref)


def source_pair_kernel(scale, width, src_ref, a_ref, gw_ref, gc_ref, out_ref, x_ref, q_ref, bd_ref, bp_ref, sum_ref):
    count, features, _ = src_ref.shape
    rank = gc_ref.shape[0]
    for b in range(count):
        x, q = unpack(src_ref[b].astype(F32), rank, width)
        x_ref[:, b * width : (b + 1) * width] = x
        q_ref[:, b * width : (b + 1) * width] = q
    lanes = x_ref.shape[1]
    put_lanes(slice(None), x_ref[...], q_ref[...], bd_ref, bp_ref)
    gw = gw_ref[...]
    gc = gc_ref[...]
    step = lanes // 2
    for start in range(0, lanes, step):
        at = slice(start, start + step)
        sum_w, sum_c = pair_sums(a_ref, gw, gc, bd_ref[:, at], bp_ref[:, at], 1024)
        sum_ref[:features, at] = feature_gradient(x_ref[:, at], sum_w, scale)
        sum_ref[features:, at] = sum_c * scale
    for b in range(count):
        block = sum_ref[:, b * width : (b + 1) * width]
        out_ref[b] = pack(block[:features], block[features:]).astype(out_ref.dtype)


def target_chunks(scale, inverse_ref, from_ref, a_ref, gw, gc, bd_ref, bp_ref, to_ref):
    count, rows, width = from_ref.shape
    features = rows - gc.shape[0]
    factor_scale = inverse_ref[...] * scale
    group = 8
    step = group * width

    def advance(index, carry):
        at = pl.ds(pl.multiple_of(index * step, step), step)
        sum_w, sum_c = pair_sums(a_ref, gw, gc, bd_ref[:, at], bp_ref[:, at], a_ref.shape[0] // 2)
        for k in range(group):
            lanes = slice(k * width, (k + 1) * width)
            x = from_ref[index * group + k][:features].astype(F32)
            grad = feature_gradient(x, sum_w[:, lanes], scale)
            to_ref[index * group + k] = jnp.concatenate([grad, sum_c[:, lanes] * factor_scale], 0)
        return carry

    lax.fori_loop(0, count // group, advance, 0)


def first_target_kernel(scale, src_width, inverse_ref, src_ref, tgt_ref, bd_ref, bp_ref, out_ref, a_ref, gw_ref, gc_ref, gw32_ref, gc32_ref):
    src_count = src_ref.shape[0]
    rank = gc_ref.shape[0]
    for b in range(src_count):
        x, q = unpack(src_ref[b].astype(F32), rank, src_width)
        put_sublanes(pl.ds(b * src_width, src_width), x, q, a_ref, gw32_ref, gc32_ref)
    gw_ref[...] = gw32_ref[...].astype(BF16)
    gc_ref[...] = gc32_ref[...].astype(BF16)
    target_chunks(scale, inverse_ref, tgt_ref, a_ref, gw_ref[...], gc_ref[...], bd_ref, bp_ref, out_ref)


def second_target_kernel(scale, inverse_ref, tgt_ref, bd_ref, bp_ref, a_ref, gw_ref, gc_ref, out_ref):
    target_chunks(scale, inverse_ref, tgt_ref, a_ref, gw_ref[...], gc_ref[...], bd_ref, bp_ref, out_ref)


def target_sum_kernel(features, parts_ref, feats_ref, factor_ref):
    total = jnp.sum(parts_ref[...].astype(F32), 0)
    feats_ref[...] = total[:features]
    factor_ref[...] = total[features:]


def source_sum_kernel(parts_ref, feats_ref, factor_ref):
    rank, width = factor_ref.shape
    feats, factor = unpack(jnp.sum(parts_ref[...].astype(F32), 0), rank, width)
    feats_ref[...] = feats
    factor_ref[...] = factor


def call(kernel, specs, outs, scratch=(), flops=0):
    single = not isinstance(outs, tuple)
    return pl.pallas_call(
        kernel,
        out_shape=outs,
        in_specs=specs,
        out_specs=VMEM if single else tuple(VMEM for _ in outs),
        scratch_shapes=scratch,
        compiler_params=pltpu.CompilerParams(vmem_limit_bytes=40 << 20),
        cost_estimate=pl.CostEstimate(flops=flops, transcendentals=0, bytes_accessed=1 << 20),
    )


def shape(*dims, dtype=F32):
    return jax.ShapeDtypeStruct(dims, dtype)


def exchange(blocks, axes):
    return lax.all_to_all(blocks, axes, 0, 0, tiled=True)


def swap(blocks):
    return lax.ppermute(blocks, CORE, [(0, 1), (1, 0)])


def local(src_feats, src_factor, tgt_feats, tgt_factor, rank_weight):
    features, src_width = src_feats.shape
    rank = src_factor.shape[0]
    rows = features + rank
    tgt_width = tgt_feats.shape[1]
    ring = lax.axis_size(RING)
    plane = lax.axis_size(PLANE)
    scale = 1.0 / (tgt_width * ring * plane * lax.axis_size(CORE))
    sources = ring * src_width
    targets = 2 * plane * tgt_width

    tgt_copies, inverse_g = call(
        target_copies_kernel,
        (HBM,) * 3,
        (shape(plane, rows, tgt_width, dtype=BF16), shape(rank, tgt_width)),
        (
            pltpu.SMEM((rank,), F32),
            pltpu.VMEM((features, tgt_width), BF16),
            pltpu.VMEM((rank, tgt_width), BF16),
            pltpu.SemaphoreType.DMA((3,)),
        ),
    )(*(pltpu.with_memory_space_constraint(array, pltpu.HBM) for array in (rank_weight, tgt_feats, tgt_factor)))
    src_copies = call(source_copies_kernel, (VMEM, VMEM), shape(ring, features, LANES, dtype=BF16))(
        src_feats, src_factor
    )
    tgt_own = exchange(tgt_copies, PLANE)
    tgt_own, src_copies = lax.optimization_barrier((tgt_own, src_copies))
    src_blocks = exchange(src_copies, RING)
    tgt_other = swap(tgt_own)

    half = plane * tgt_width
    a, gw, gc, own_bd, own_bp, other_bd, other_bp = call(
        lambda *refs: target_prepare_kernel(features, *refs),
        (VMEM, VMEM),
        (
            shape(targets, 64, dtype=BF16),
            shape(features + 8, targets, dtype=BF16),
            shape(rank, targets, dtype=BF16),
        )
        + (shape(64, half, dtype=BF16),) * 4,
        flops=1 << 22,
    )(tgt_own, tgt_other)

    flops = sources * targets * 2 * 256 * 4
    src_parts = call(
        lambda *refs: source_pair_kernel(scale, src_width, *refs),
        (VMEM,) * 4,
        shape(ring, features, LANES, dtype=BF16),
        (
            pltpu.VMEM((features, sources), F32),
            pltpu.VMEM((rank, sources), F32),
            pltpu.VMEM((64, sources), BF16),
            pltpu.VMEM((64, sources), BF16),
            pltpu.VMEM((rows, sources), F32),
        ),
        flops,
    )(src_blocks, a, gw, gc)
    src_sums = exchange(src_parts, RING)
    send, src_a, src_gw, src_gc = call(
        lambda *refs: first_target_kernel(scale, src_width, *refs),
        (VMEM,) * 5,
        (
            shape(plane, rows, tgt_width),
            shape(sources, 64, dtype=BF16),
            shape(features + 8, sources, dtype=BF16),
            shape(rank, sources, dtype=BF16),
        ),
        (pltpu.VMEM((features + 8, sources), F32), pltpu.VMEM((rank, sources), F32)),
        flops // 2,
    )(inverse_g, src_blocks, tgt_other, other_bd, other_bp)
    received = swap(send)
    keep = call(
        lambda *refs: second_target_kernel(scale, *refs),
        (VMEM,) * 7,
        shape(plane, rows, tgt_width),
        flops=flops // 2,
    )(inverse_g, tgt_own, own_bd, own_bp, src_a, src_gw, src_gc)
    src_sums, tgt_half = lax.optimization_barrier((src_sums, (keep + received).astype(BF16)))
    tgt_sums = exchange(tgt_half, PLANE)

    grad_x, grad_q = call(source_sum_kernel, (VMEM,), (shape(features, src_width), shape(rank, src_width)))(src_sums)
    grad_y, grad_r = call(
        lambda *refs: target_sum_kernel(features, *refs), (VMEM,), (shape(features, tgt_width), shape(rank, tgt_width))
    )(tgt_sums)
    return grad_x, grad_q, grad_y, grad_r


def solution(mesh):
    fine = Mesh(mesh.devices.reshape(8, 2, 2, 4, 4), ("zl", "core", "zh", "y", "x"))
    by_src = P(None, ("zl", "core", "zh", "y", "x"))
    by_tgt = P(None, ("zh", "y", "x", "zl", "core"))
    return jax.shard_map(
        local,
        mesh=fine,
        in_specs=(by_src, by_src, by_tgt, by_tgt, P()),
        out_specs=(by_src, by_src, by_tgt, by_tgt),
        check_vma=False,
    )
```

```python
import jax
import jax.numpy as jnp
from jax import lax
from jax.experimental import pallas as pl
from jax.experimental.pallas import tpu as pltpu
from jax.sharding import Mesh
from jax.sharding import PartitionSpec as P

RING = ("zh", "zl")
PLANE = ("y", "x")
CORE = "core"
BF16 = jnp.bfloat16
F32 = jnp.float32
VMEM = pl.BlockSpec(memory_space=pltpu.VMEM)
HBM = pl.BlockSpec(memory_space=pltpu.HBM)
LANES = 128


def dot(a, b):
    return jnp.dot(a, b, preferred_element_type=F32)


def inverse_column(rank_ref, width):
    rank = rank_ref.shape[0]
    rows = lax.broadcasted_iota(jnp.int32, (rank, width), 0)
    column = jnp.full((rank, width), rank_ref[0], F32)
    for k in range(1, rank):
        column = jnp.where(rows == k, rank_ref[k], column)
    return 1.0 / column


def pack(feats, factor):
    rows, width = feats.shape
    half = width // 2
    halves = jnp.concatenate([factor[:, :half], factor[:, half:]], 0)
    return jnp.concatenate([feats, halves, jnp.zeros((rows, LANES - width - half), F32)], 1)


def unpack(block, rank, width):
    half = width // 2
    halves = block[:, width : width + half]
    return block[:, :width], jnp.concatenate([halves[:rank], halves[rank:]], 1)


def load_all(pairs, sems):
    loads = [pltpu.make_async_copy(a, b, sems.at[k]) for k, (a, b) in enumerate(pairs)]
    for load in loads:
        load.start()
    for load in loads:
        load.wait()


def source_copies_kernel(feats_hbm, factor_hbm, out_ref, feats_ref, factor_ref, sems):
    load_all([(feats_hbm, feats_ref), (factor_hbm, factor_ref)], sems)
    block = pack(feats_ref[...].astype(F32), factor_ref[...].astype(F32)).astype(BF16)
    for member in range(out_ref.shape[0]):
        out_ref[member] = block


def target_block_kernel(rank_hbm, feats_hbm, factor_hbm, out_ref, inverse_ref, rank_ref, feats_ref, factor_ref, sems):
    load_all([(rank_hbm, rank_ref), (feats_hbm, feats_ref), (factor_hbm, factor_ref)], sems)
    factor = factor_ref[...]
    inverse_g = inverse_column(rank_ref, factor.shape[1])
    inverse_ref[...] = inverse_g
    scaled = (factor.astype(F32) * inverse_g).astype(BF16)
    out_ref[...] = jnp.concatenate([feats_ref[...], scaled], 0)


def target_copies_kernel(own_ref, other_ref, out_ref):
    own = own_ref[...]
    other = other_ref[...]
    for member in range(out_ref.shape[0]):
        out_ref[member, 0] = own
        out_ref[member, 1] = other


def three_parts(value):
    high = value.astype(BF16).astype(F32)
    rest = value - high
    mid = rest.astype(BF16).astype(F32)
    low = (rest - mid).astype(BF16).astype(F32)
    return [high, mid, low]


def squares(feats):
    return jnp.sum(jnp.square(feats), 0, keepdims=True)


def put_sublanes(at, x, q, a_ref, gw_ref, gc_ref):
    width = x.shape[1]
    ones = jnp.ones((1, width), F32)
    stack = jnp.concatenate(
        [-2.0 * x, q] + three_parts(squares(x)) + [ones] * 3 + [jnp.zeros((10, width), F32)], 0
    )
    a_ref[at, :] = stack.T.astype(BF16)
    gw_ref[:, at] = jnp.concatenate([x, ones, jnp.zeros((7, width), F32)], 0).astype(gw_ref.dtype)
    gc_ref[:, at] = q.astype(gc_ref.dtype)


def put_lanes(at, x, q, bd_ref, bp_ref):
    features, width = x.shape
    rank = q.shape[0]
    bd_ref[:, at] = jnp.concatenate(
        [x, jnp.zeros((rank, width), F32), jnp.ones((3, width), F32)]
        + three_parts(squares(x) + 1.0)
        + [jnp.zeros((10, width), F32)],
        0,
    ).astype(BF16)
    bp_ref[:, at] = jnp.concatenate(
        [jnp.zeros((features, width), F32), q, jnp.zeros((16, width), F32)], 0
    ).astype(BF16)


def pair_sums(a_ref, gw, gc, bd, bp, step):
    lanes = bd.shape[1]
    sum_w = jnp.zeros((gw.shape[0], lanes), F32)
    sum_c = jnp.zeros((gc.shape[0], lanes), F32)
    for u in range(0, a_ref.shape[0], step):
        a = a_ref[pl.ds(u, step), :]
        s = dot(a, bd)
        p = dot(a, bp)
        r = lax.rsqrt(s)
        sum_w += dot(gw[:, u : u + step], (p * r).astype(BF16))
        sum_c += dot(gc[:, u : u + step], (s * r).astype(BF16))
    return sum_w, sum_c


def feature_gradient(x, sum_w, scale):
    features = x.shape[0]
    return (x * sum_w[features : features + 1] - sum_w[:features]) * scale


def source_prepare_kernel(width, src_ref, x_ref, bd_ref, bp_ref, a_ref, gw_ref, gc_ref, q32_ref, gw32_ref, gc32_ref):
    rank = gc_ref.shape[0]
    for b in range(src_ref.shape[0]):
        x, q = unpack(src_ref[b].astype(F32), rank, width)
        at = pl.ds(b * width, width)
        x_ref[:, at] = x
        q32_ref[:, at] = q
        put_sublanes(at, x, q, a_ref, gw32_ref, gc32_ref)
    gw_ref[...] = gw32_ref[...].astype(BF16)
    gc_ref[...] = gc32_ref[...].astype(BF16)
    put_lanes(slice(None), x_ref[...], q32_ref[...], bd_ref, bp_ref)


def source_pair_kernel(scale, width, tgt_ref, x_ref, bd_ref, bp_ref, out_ref, a_ref, gw_ref, gc_ref, sum_ref):
    features = x_ref.shape[0]
    count, _, _, tgt_width = tgt_ref.shape
    for b in range(2 * count):
        block = tgt_ref[b // 2, b % 2].astype(F32)
        put_sublanes(pl.ds(b * tgt_width, tgt_width), block[:features], block[features:], a_ref, gw_ref, gc_ref)
    lanes = x_ref.shape[1]
    gw = gw_ref[...]
    gc = gc_ref[...]
    step = lanes // 2
    for start in range(0, lanes, step):
        at = slice(start, start + step)
        sum_w, sum_c = pair_sums(a_ref, gw, gc, bd_ref[:, at], bp_ref[:, at], 1024)
        sum_ref[:features, at] = feature_gradient(x_ref[:, at], sum_w, scale)
        sum_ref[features:, at] = sum_c * scale
    for b in range(out_ref.shape[0]):
        block = sum_ref[:, b * width : (b + 1) * width]
        out_ref[b] = pack(block[:features], block[features:]).astype(out_ref.dtype)


def target_pair_kernel(scale, half, inverse_ref, tgt_ref, a_ref, gw_ref, gc_ref, out_ref, bd_ref, bp_ref):
    count, _, rows, width = tgt_ref.shape
    features = rows - gc_ref.shape[0]
    for b in range(count):
        block = tgt_ref[b, half].astype(F32)
        put_lanes(pl.ds(b * width, width), block[:features], block[features:], bd_ref, bp_ref)
    gw = gw_ref[...]
    gc = gc_ref[...]
    factor_scale = inverse_ref[...] * scale
    group = 8
    step = group * width

    def advance(index, carry):
        at = pl.ds(pl.multiple_of(index * step, step), step)
        sum_w, sum_c = pair_sums(a_ref, gw, gc, bd_ref[:, at], bp_ref[:, at], a_ref.shape[0] // 2)
        for k in range(group):
            lanes = slice(k * width, (k + 1) * width)
            x = tgt_ref[index * group + k, half][:features].astype(F32)
            grad = feature_gradient(x, sum_w[:, lanes], scale)
            out_ref[index * group + k] = jnp.concatenate([grad, sum_c[:, lanes] * factor_scale], 0)
        return carry

    lax.fori_loop(0, count // group, advance, 0)


def target_sum_kernel(features, parts_ref, feats_ref, factor_ref):
    total = jnp.sum(parts_ref[...].astype(F32), 0)
    feats_ref[...] = total[:features]
    factor_ref[...] = total[features:]


def source_sum_kernel(parts_ref, feats_ref, factor_ref):
    rank, width = factor_ref.shape
    feats, factor = unpack(jnp.sum(parts_ref[...].astype(F32), 0), rank, width)
    feats_ref[...] = feats
    factor_ref[...] = factor


def call(kernel, specs, outs, scratch=(), flops=0):
    single = not isinstance(outs, tuple)
    return pl.pallas_call(
        kernel,
        out_shape=outs,
        in_specs=specs,
        out_specs=VMEM if single else tuple(VMEM for _ in outs),
        scratch_shapes=scratch,
        compiler_params=pltpu.CompilerParams(vmem_limit_bytes=40 << 20),
        cost_estimate=pl.CostEstimate(flops=flops, transcendentals=0, bytes_accessed=1 << 20),
    )


def shape(*dims, dtype=F32):
    return jax.ShapeDtypeStruct(dims, dtype)


def exchange(blocks, axes):
    return lax.all_to_all(blocks, axes, 0, 0, tiled=True)


def in_hbm(array):
    return pltpu.with_memory_space_constraint(array, pltpu.HBM)


def swap(blocks):
    return lax.ppermute(blocks, CORE, [(0, 1), (1, 0)])


def local(src_feats, src_factor, tgt_feats, tgt_factor, rank_weight):
    features, src_width = src_feats.shape
    rank = src_factor.shape[0]
    rows = features + rank
    tgt_width = tgt_feats.shape[1]
    ring = lax.axis_size(RING)
    plane = lax.axis_size(PLANE)
    scale = 1.0 / (tgt_width * ring * plane * lax.axis_size(CORE))
    sources = ring * src_width
    targets = 2 * plane * tgt_width

    src_copies = call(
        source_copies_kernel,
        (HBM,) * 2,
        shape(ring, features, LANES, dtype=BF16),
        (
            pltpu.VMEM((features, src_width), BF16),
            pltpu.VMEM((rank, src_width), BF16),
            pltpu.SemaphoreType.DMA((2,)),
        ),
    )(*map(in_hbm, (src_feats, src_factor)))
    src_blocks = exchange(src_copies, RING)
    tgt_own, inverse_g = call(
        target_block_kernel,
        (HBM,) * 3,
        (shape(rows, tgt_width, dtype=BF16), shape(rank, tgt_width)),
        (
            pltpu.SMEM((rank,), F32),
            pltpu.VMEM((features, tgt_width), BF16),
            pltpu.VMEM((rank, tgt_width), BF16),
            pltpu.SemaphoreType.DMA((3,)),
        ),
    )(*map(in_hbm, (rank_weight, tgt_feats, tgt_factor)))
    tgt_copies = call(target_copies_kernel, (VMEM, VMEM), shape(plane, 2, rows, tgt_width, dtype=BF16))(
        tgt_own, swap(tgt_own)
    )
    src_blocks, tgt_copies = lax.optimization_barrier((src_blocks, tgt_copies))
    tgt_blocks = exchange(tgt_copies, PLANE)

    x, bd, bp, a, gw, gc = call(
        lambda *refs: source_prepare_kernel(src_width, *refs),
        (VMEM,),
        (
            shape(features, sources),
            shape(64, sources, dtype=BF16),
            shape(64, sources, dtype=BF16),
            shape(sources, 64, dtype=BF16),
            shape(features + 8, sources, dtype=BF16),
            shape(rank, sources, dtype=BF16),
        ),
        (
            pltpu.VMEM((rank, sources), F32),
            pltpu.VMEM((features + 8, sources), F32),
            pltpu.VMEM((rank, sources), F32),
        ),
        flops=1 << 22,
    )(src_blocks)

    flops = sources * targets * 2 * 256 * 4
    src_parts = call(
        lambda *refs: source_pair_kernel(scale, src_width, *refs),
        (VMEM,) * 4,
        shape(ring, features, LANES, dtype=BF16),
        (
            pltpu.VMEM((targets, 64), BF16),
            pltpu.VMEM((features + 8, targets), BF16),
            pltpu.VMEM((rank, targets), BF16),
            pltpu.VMEM((rows, sources), F32),
        ),
        flops,
    )(tgt_blocks, x, bd, bp)
    src_sums = exchange(src_parts, RING)

    def target_half(half):
        return call(
            lambda *refs: target_pair_kernel(scale, half, *refs),
            (VMEM,) * 5,
            shape(plane, rows, tgt_width),
            (pltpu.VMEM((64, targets // 2), BF16), pltpu.VMEM((64, targets // 2), BF16)),
            flops // 2,
        )(inverse_g, tgt_blocks, a, gw, gc)

    received = swap(target_half(1))
    keep = target_half(0)
    src_sums, tgt_half = lax.optimization_barrier((src_sums, (keep + received).astype(BF16)))
    tgt_sums = exchange(tgt_half, PLANE)

    grad_x, grad_q = call(source_sum_kernel, (VMEM,), (shape(features, src_width), shape(rank, src_width)))(src_sums)
    grad_y, grad_r = call(
        lambda *refs: target_sum_kernel(features, *refs), (VMEM,), (shape(features, tgt_width), shape(rank, tgt_width))
    )(tgt_sums)
    return grad_x, grad_q, grad_y, grad_r


def solution(mesh):
    fine = Mesh(mesh.devices.reshape(8, 2, 2, 4, 4), ("zl", "core", "zh", "y", "x"))
    by_src = P(None, ("zl", "core", "zh", "y", "x"))
    by_tgt = P(None, ("zh", "y", "x", "zl", "core"))
    return jax.shard_map(
        local,
        mesh=fine,
        in_specs=(by_src, by_src, by_tgt, by_tgt, P()),
        out_specs=(by_src, by_src, by_tgt, by_tgt),
        check_vma=False,
    )
```

```python
import jax
import jax.numpy as jnp
from jax import lax
from jax.experimental import pallas as pl
from jax.experimental.pallas import tpu as pltpu
from jax.sharding import Mesh
from jax.sharding import PartitionSpec as P

RING = ("zh", "zl")
PLANE = ("y", "x")
CORE = "core"
BF16 = jnp.bfloat16
F32 = jnp.float32
VMEM = pl.BlockSpec(memory_space=pltpu.VMEM)
HBM = pl.BlockSpec(memory_space=pltpu.HBM)
LANES = 128


def dot(a, b):
    return jnp.dot(a, b, preferred_element_type=F32)


def inverse_column(rank_ref, width):
    rank = rank_ref.shape[0]
    rows = lax.broadcasted_iota(jnp.int32, (rank, width), 0)
    column = jnp.full((rank, width), rank_ref[0], F32)
    for k in range(1, rank):
        column = jnp.where(rows == k, rank_ref[k], column)
    return 1.0 / column


def pack(feats, factor):
    rows, width = feats.shape
    half = width // 2
    halves = jnp.concatenate([factor[:, :half], factor[:, half:]], 0)
    return jnp.concatenate([feats, halves, jnp.zeros((rows, LANES - width - half), F32)], 1)


def unpack(block, rank, width):
    half = width // 2
    halves = block[:, width : width + half]
    return block[:, :width], jnp.concatenate([halves[:rank], halves[rank:]], 1)


def source_copies_kernel(feats_ref, factor_ref, out_ref):
    block = pack(feats_ref[...].astype(F32), factor_ref[...].astype(F32)).astype(BF16)
    for member in range(out_ref.shape[0]):
        out_ref[member] = block


def target_copies_kernel(rank_hbm, feats_hbm, factor_hbm, out_ref, inverse_ref, rank_ref, feats_ref, factor_ref, sems):
    pairs = [(rank_hbm, rank_ref), (feats_hbm, feats_ref), (factor_hbm, factor_ref)]
    loads = [pltpu.make_async_copy(a, b, sems.at[k]) for k, (a, b) in enumerate(pairs)]
    for load in loads:
        load.start()
    for load in loads:
        load.wait()
    factor = factor_ref[...]
    inverse_g = inverse_column(rank_ref, factor.shape[1])
    inverse_ref[...] = inverse_g
    scaled = (factor.astype(F32) * inverse_g).astype(BF16)
    block = jnp.concatenate([feats_ref[...], scaled], 0)
    for member in range(out_ref.shape[0]):
        out_ref[member] = block


def three_parts(value):
    high = value.astype(BF16).astype(F32)
    rest = value - high
    mid = rest.astype(BF16).astype(F32)
    low = (rest - mid).astype(BF16).astype(F32)
    return [high, mid, low]


def squares(feats):
    return jnp.sum(jnp.square(feats), 0, keepdims=True)


def put_sublanes(at, x, q, a_ref, gw_ref, gc_ref):
    width = x.shape[1]
    ones = jnp.ones((1, width), F32)
    stack = jnp.concatenate(
        [-2.0 * x, q] + three_parts(squares(x)) + [ones] * 3 + [jnp.zeros((10, width), F32)], 0
    )
    a_ref[at, :] = stack.T.astype(BF16)
    gw_ref[:, at] = jnp.concatenate([x, ones, jnp.zeros((7, width), F32)], 0).astype(BF16)
    gc_ref[:, at] = q.astype(BF16)


def lane_operands(x, q):
    features, width = x.shape
    rank = q.shape[0]
    distance = jnp.concatenate(
        [x, jnp.zeros((rank, width), F32), jnp.ones((3, width), F32)]
        + three_parts(squares(x) + 1.0)
        + [jnp.zeros((10, width), F32)],
        0,
    )
    plan = jnp.concatenate([jnp.zeros((features, width), F32), q, jnp.zeros((16, width), F32)], 0)
    return distance.astype(BF16), plan.astype(BF16)


def pair_sums(a_ref, gw, gc, bd, bp, step):
    lanes = bd.shape[1]
    sum_w = jnp.zeros((gw.shape[0], lanes), F32)
    sum_c = jnp.zeros((gc.shape[0], lanes), F32)
    for u in range(0, a_ref.shape[0], step):
        a = a_ref[pl.ds(u, step), :]
        s = dot(a, bd)
        p = dot(a, bp)
        r = lax.rsqrt(s)
        sum_w += dot(gw[:, u : u + step], (p * r).astype(BF16))
        sum_c += dot(gc[:, u : u + step], (s * r).astype(BF16))
    return sum_w, sum_c


def feature_gradient(x, sum_w, scale):
    features = x.shape[0]
    return (x * sum_w[features : features + 1] - sum_w[:features]) * scale


def target_prepare_kernel(features, own_ref, other_ref, a_ref, gw_ref, gc_ref, own_bd, own_bp, other_bd, other_bp):
    count, _, width = own_ref.shape
    for half, (ref, bd_ref, bp_ref) in enumerate([(own_ref, own_bd, own_bp), (other_ref, other_bd, other_bp)]):
        for b in range(count):
            block = ref[b].astype(F32)
            put_sublanes(
                pl.ds((half * count + b) * width, width), block[:features], block[features:], a_ref, gw_ref, gc_ref
            )
            lanes = pl.ds(b * width, width)
            bd_ref[:, lanes], bp_ref[:, lanes] = lane_operands(block[:features], block[features:])


def source_pair_kernel(scale, width, src_ref, a_ref, gw_ref, gc_ref, out_ref, all_ref, bd_ref, bp_ref, sum_ref):
    count, features, _ = src_ref.shape
    rank = gc_ref.shape[0]
    for b in range(count):
        lanes = slice(b * width, (b + 1) * width)
        all_ref[:features, lanes], all_ref[features:, lanes] = unpack(src_ref[b].astype(F32), rank, width)
    bd_ref[...], bp_ref[...] = lane_operands(all_ref[:features], all_ref[features:])
    gw = gw_ref[...]
    gc = gc_ref[...]
    total = all_ref.shape[1]
    step = total // 2
    for start in range(0, total, step):
        at = slice(start, start + step)
        sum_w, sum_c = pair_sums(a_ref, gw, gc, bd_ref[:, at], bp_ref[:, at], 1024)
        sum_ref[:features, at] = feature_gradient(all_ref[:features, at], sum_w, scale)
        sum_ref[features:, at] = sum_c * scale
    for b in range(count):
        block = sum_ref[:, b * width : (b + 1) * width]
        out_ref[b] = pack(block[:features], block[features:]).astype(out_ref.dtype)


def target_chunks(scale, inverse_ref, from_ref, a_ref, gw, gc, bd_ref, bp_ref, to_ref):
    count, rows, width = from_ref.shape
    features = rows - gc.shape[0]
    factor_scale = inverse_ref[...] * scale
    group = 8
    step = group * width

    def advance(index, carry):
        at = pl.ds(pl.multiple_of(index * step, step), step)
        sum_w, sum_c = pair_sums(a_ref, gw, gc, bd_ref[:, at], bp_ref[:, at], a_ref.shape[0] // 2)
        for k in range(group):
            lanes = slice(k * width, (k + 1) * width)
            x = from_ref[index * group + k][:features].astype(F32)
            grad = feature_gradient(x, sum_w[:, lanes], scale)
            to_ref[index * group + k] = jnp.concatenate([grad, sum_c[:, lanes] * factor_scale], 0)
        return carry

    lax.fori_loop(0, count // group, advance, 0)


def first_target_kernel(scale, features, inverse_ref, src_ref, tgt_ref, bd_ref, bp_ref, out_ref, a_ref, gw_ref, gc_ref):
    put_sublanes(slice(None), src_ref[:features], src_ref[features:], a_ref, gw_ref, gc_ref)
    target_chunks(scale, inverse_ref, tgt_ref, a_ref, gw_ref[...], gc_ref[...], bd_ref, bp_ref, out_ref)


def second_target_kernel(scale, inverse_ref, tgt_ref, bd_ref, bp_ref, a_ref, gw_ref, gc_ref, out_ref):
    target_chunks(scale, inverse_ref, tgt_ref, a_ref, gw_ref[...], gc_ref[...], bd_ref, bp_ref, out_ref)


def add_kernel(a_ref, b_ref, out_ref):
    out_ref[...] = (a_ref[...] + b_ref[...]).astype(out_ref.dtype)


def target_sum_kernel(features, parts_ref, feats_ref, factor_ref):
    total = jnp.sum(parts_ref[...].astype(F32), 0)
    feats_ref[...] = total[:features]
    factor_ref[...] = total[features:]


def source_sum_kernel(parts_ref, feats_ref, factor_ref):
    rank, width = factor_ref.shape
    feats, factor = unpack(jnp.sum(parts_ref[...].astype(F32), 0), rank, width)
    feats_ref[...] = feats
    factor_ref[...] = factor


def call(kernel, specs, outs, scratch=(), flops=0):
    single = not isinstance(outs, tuple)
    return pl.pallas_call(
        kernel,
        out_shape=outs,
        in_specs=specs,
        out_specs=VMEM if single else tuple(VMEM for _ in outs),
        scratch_shapes=scratch,
        compiler_params=pltpu.CompilerParams(vmem_limit_bytes=40 << 20),
        cost_estimate=pl.CostEstimate(flops=flops, transcendentals=0, bytes_accessed=1 << 20),
    )


def shape(*dims, dtype=F32):
    return jax.ShapeDtypeStruct(dims, dtype)


def exchange(blocks, axes):
    return lax.all_to_all(blocks, axes, 0, 0, tiled=True)


def swap(blocks):
    return lax.ppermute(blocks, CORE, [(0, 1), (1, 0)])


def local(src_feats, src_factor, tgt_feats, tgt_factor, rank_weight):
    features, src_width = src_feats.shape
    rank = src_factor.shape[0]
    rows = features + rank
    tgt_width = tgt_feats.shape[1]
    ring = lax.axis_size(RING)
    plane = lax.axis_size(PLANE)
    scale = 1.0 / (tgt_width * ring * plane * lax.axis_size(CORE))
    sources = ring * src_width
    targets = 2 * plane * tgt_width

    tgt_copies, inverse_g = call(
        target_copies_kernel,
        (HBM,) * 3,
        (shape(plane, rows, tgt_width, dtype=BF16), shape(rank, tgt_width)),
        (
            pltpu.SMEM((rank,), F32),
            pltpu.VMEM((features, tgt_width), BF16),
            pltpu.VMEM((rank, tgt_width), BF16),
            pltpu.SemaphoreType.DMA((3,)),
        ),
    )(*(pltpu.with_memory_space_constraint(array, pltpu.HBM) for array in (rank_weight, tgt_feats, tgt_factor)))
    src_copies = call(source_copies_kernel, (VMEM, VMEM), shape(ring, features, LANES, dtype=BF16))(
        src_feats, src_factor
    )
    tgt_own = exchange(tgt_copies, PLANE)
    tgt_own, src_copies = lax.optimization_barrier((tgt_own, src_copies))
    src_blocks = exchange(src_copies, RING)
    tgt_other = swap(tgt_own)

    half = plane * tgt_width
    a, gw, gc, own_bd, own_bp, other_bd, other_bp = call(
        lambda *refs: target_prepare_kernel(features, *refs),
        (VMEM, VMEM),
        (
            shape(targets, 64, dtype=BF16),
            shape(features + 8, targets, dtype=BF16),
            shape(rank, targets, dtype=BF16),
        )
        + (shape(64, half, dtype=BF16),) * 4,
        flops=1 << 22,
    )(tgt_own, tgt_other)

    flops = sources * targets * 2 * 256 * 4
    src_parts, src_all = call(
        lambda *refs: source_pair_kernel(scale, src_width, *refs),
        (VMEM,) * 4,
        (shape(ring, features, LANES, dtype=BF16), shape(rows, sources)),
        (
            pltpu.VMEM((64, sources), BF16),
            pltpu.VMEM((64, sources), BF16),
            pltpu.VMEM((rows, sources), F32),
        ),
        flops,
    )(src_blocks, a, gw, gc)
    src_sums = exchange(src_parts, RING)
    send, src_a, src_gw, src_gc = call(
        lambda *refs: first_target_kernel(scale, features, *refs),
        (VMEM,) * 5,
        (
            shape(plane, rows, tgt_width),
            shape(sources, 64, dtype=BF16),
            shape(features + 8, sources, dtype=BF16),
            shape(rank, sources, dtype=BF16),
        ),
        flops=flops // 2,
    )(inverse_g, src_all, tgt_other, other_bd, other_bp)
    received = swap(send)
    keep = call(
        lambda *refs: second_target_kernel(scale, *refs),
        (VMEM,) * 7,
        shape(plane, rows, tgt_width),
        flops=flops // 2,
    )(inverse_g, tgt_own, own_bd, own_bp, src_a, src_gw, src_gc)
    tgt_half = call(add_kernel, (VMEM, VMEM), shape(plane, rows, tgt_width, dtype=BF16))(keep, received)
    src_sums, tgt_half = lax.optimization_barrier((src_sums, tgt_half))
    tgt_sums = exchange(tgt_half, PLANE)

    grad_x, grad_q = call(source_sum_kernel, (VMEM,), (shape(features, src_width), shape(rank, src_width)))(src_sums)
    grad_y, grad_r = call(
        lambda *refs: target_sum_kernel(features, *refs), (VMEM,), (shape(features, tgt_width), shape(rank, tgt_width))
    )(tgt_sums)
    return grad_x, grad_q, grad_y, grad_r


def solution(mesh):
    fine = Mesh(mesh.devices.reshape(8, 2, 2, 4, 4), ("zl", "core", "zh", "y", "x"))
    by_src = P(None, ("zl", "core", "zh", "y", "x"))
    by_tgt = P(None, ("zh", "y", "x", "zl", "core"))
    return jax.shard_map(
        local,
        mesh=fine,
        in_specs=(by_src, by_src, by_tgt, by_tgt, P()),
        out_specs=(by_src, by_src, by_tgt, by_tgt),
        check_vma=False,
    )
```

```python
import jax
import jax.numpy as jnp
from jax import lax
from jax.experimental import pallas as pl
from jax.experimental.pallas import tpu as pltpu
from jax.sharding import Mesh
from jax.sharding import PartitionSpec as P

RING = ("zh", "zl")
PLANE = ("y", "x")
CORE = "core"
BF16 = jnp.bfloat16
F32 = jnp.float32
VMEM = pl.BlockSpec(memory_space=pltpu.VMEM)
HBM = pl.BlockSpec(memory_space=pltpu.HBM)
LANES = 128


def dot(a, b):
    return jnp.dot(a, b, preferred_element_type=F32)


def inverse_column(rank_ref, width):
    rank = rank_ref.shape[0]
    rows = lax.broadcasted_iota(jnp.int32, (rank, width), 0)
    column = jnp.full((rank, width), rank_ref[0], F32)
    for k in range(1, rank):
        column = jnp.where(rows == k, rank_ref[k], column)
    return 1.0 / column


def pack(feats, factor):
    rows, width = feats.shape
    half = width // 2
    halves = jnp.concatenate([factor[:, :half], factor[:, half:]], 0)
    return jnp.concatenate([feats, halves, jnp.zeros((rows, LANES - width - half), F32)], 1)


def unpack(block, rank, width):
    half = width // 2
    halves = block[:, width : width + half]
    return block[:, :width], jnp.concatenate([halves[:rank], halves[rank:]], 1)


def copies_kernel(rank_hbm, tgt_hbm, tgt_factor_hbm, src_hbm, src_factor_hbm, tgt_out, src_out, inverse_ref, rank_ref, tgt_ref, tgt_factor_ref, src_ref, src_factor_ref, sems):
    pairs = [
        (rank_hbm, rank_ref),
        (tgt_hbm, tgt_ref),
        (tgt_factor_hbm, tgt_factor_ref),
        (src_hbm, src_ref),
        (src_factor_hbm, src_factor_ref),
    ]
    loads = [pltpu.make_async_copy(a, b, sems.at[k]) for k, (a, b) in enumerate(pairs)]
    for load in loads:
        load.start()
    for load in loads:
        load.wait()
    factor = tgt_factor_ref[...]
    inverse_g = inverse_column(rank_ref, factor.shape[1])
    inverse_ref[...] = inverse_g
    scaled = (factor.astype(F32) * inverse_g).astype(BF16)
    tgt_block = jnp.concatenate([tgt_ref[...], scaled], 0)
    for member in range(tgt_out.shape[0]):
        tgt_out[member] = tgt_block
    src_block = pack(src_ref[...].astype(F32), src_factor_ref[...].astype(F32)).astype(BF16)
    for member in range(src_out.shape[0]):
        src_out[member] = src_block


def three_parts(value):
    high = value.astype(BF16).astype(F32)
    rest = value - high
    mid = rest.astype(BF16).astype(F32)
    low = (rest - mid).astype(BF16).astype(F32)
    return [high, mid, low]


def squares(feats):
    return jnp.sum(jnp.square(feats), 0, keepdims=True)


def put_sublanes(at, x, q, a_ref, gw_ref, gc_ref):
    width = x.shape[1]
    ones = jnp.ones((1, width), F32)
    stack = jnp.concatenate(
        [-2.0 * x, q] + three_parts(squares(x)) + [ones] * 3 + [jnp.zeros((10, width), F32)], 0
    )
    a_ref[at, :] = stack.T.astype(BF16)
    gw_ref[:, at] = jnp.concatenate([x, ones, jnp.zeros((7, width), F32)], 0).astype(BF16)
    gc_ref[:, at] = q.astype(BF16)


def lane_operands(x, q):
    features, width = x.shape
    rank = q.shape[0]
    distance = jnp.concatenate(
        [x, jnp.zeros((rank, width), F32), jnp.ones((3, width), F32)]
        + three_parts(squares(x) + 1.0)
        + [jnp.zeros((10, width), F32)],
        0,
    )
    plan = jnp.concatenate([jnp.zeros((features, width), F32), q, jnp.zeros((16, width), F32)], 0)
    return distance.astype(BF16), plan.astype(BF16)


def pair_sums(a_ref, gw, gc, bd, bp, step):
    lanes = bd.shape[1]
    sum_w = jnp.zeros((gw.shape[0], lanes), F32)
    sum_c = jnp.zeros((gc.shape[0], lanes), F32)
    for u in range(0, a_ref.shape[0], step):
        a = a_ref[pl.ds(u, step), :]
        s = dot(a, bd)
        p = dot(a, bp)
        r = lax.rsqrt(s)
        sum_w += dot(gw[:, u : u + step], (p * r).astype(BF16))
        sum_c += dot(gc[:, u : u + step], (s * r).astype(BF16))
    return sum_w, sum_c


def feature_gradient(x, sum_w, scale):
    features = x.shape[0]
    return (x * sum_w[features : features + 1] - sum_w[:features]) * scale


def target_prepare_kernel(features, own_ref, other_ref, a_ref, gw_ref, gc_ref, own_bd, own_bp, other_bd, other_bp):
    count, _, width = own_ref.shape
    for half, (ref, bd_ref, bp_ref) in enumerate([(own_ref, own_bd, own_bp), (other_ref, other_bd, other_bp)]):
        for b in range(count):
            block = ref[b].astype(F32)
            put_sublanes(
                pl.ds((half * count + b) * width, width), block[:features], block[features:], a_ref, gw_ref, gc_ref
            )
            lanes = pl.ds(b * width, width)
            bd_ref[:, lanes], bp_ref[:, lanes] = lane_operands(block[:features], block[features:])


def source_pair_kernel(scale, width, src_ref, a_ref, gw_ref, gc_ref, out_ref, all_ref, bd_ref, bp_ref, sum_ref):
    count, features, _ = src_ref.shape
    rank = gc_ref.shape[0]
    for b in range(count):
        lanes = slice(b * width, (b + 1) * width)
        all_ref[:features, lanes], all_ref[features:, lanes] = unpack(src_ref[b].astype(F32), rank, width)
    bd_ref[...], bp_ref[...] = lane_operands(all_ref[:features], all_ref[features:])
    gw = gw_ref[...]
    gc = gc_ref[...]
    total = all_ref.shape[1]
    step = total // 2
    for start in range(0, total, step):
        at = slice(start, start + step)
        sum_w, sum_c = pair_sums(a_ref, gw, gc, bd_ref[:, at], bp_ref[:, at], 1024)
        sum_ref[:features, at] = feature_gradient(all_ref[:features, at], sum_w, scale)
        sum_ref[features:, at] = sum_c * scale
    for b in range(count):
        block = sum_ref[:, b * width : (b + 1) * width]
        out_ref[b] = pack(block[:features], block[features:]).astype(out_ref.dtype)


def target_chunks(scale, inverse_ref, from_ref, a_ref, gw, gc, bd_ref, bp_ref, to_ref):
    count, rows, width = from_ref.shape
    features = rows - gc.shape[0]
    factor_scale = inverse_ref[...] * scale
    group = 8
    step = group * width

    def advance(index, carry):
        at = pl.ds(pl.multiple_of(index * step, step), step)
        sum_w, sum_c = pair_sums(a_ref, gw, gc, bd_ref[:, at], bp_ref[:, at], a_ref.shape[0] // 2)
        for k in range(group):
            lanes = slice(k * width, (k + 1) * width)
            x = from_ref[index * group + k][:features].astype(F32)
            grad = feature_gradient(x, sum_w[:, lanes], scale)
            to_ref[index * group + k] = jnp.concatenate([grad, sum_c[:, lanes] * factor_scale], 0)
        return carry

    lax.fori_loop(0, count // group, advance, 0)


def first_target_kernel(scale, features, inverse_ref, src_ref, tgt_ref, bd_ref, bp_ref, out_ref, a_ref, gw_ref, gc_ref):
    put_sublanes(slice(None), src_ref[:features], src_ref[features:], a_ref, gw_ref, gc_ref)
    target_chunks(scale, inverse_ref, tgt_ref, a_ref, gw_ref[...], gc_ref[...], bd_ref, bp_ref, out_ref)


def second_target_kernel(scale, inverse_ref, tgt_ref, bd_ref, bp_ref, a_ref, gw_ref, gc_ref, out_ref):
    target_chunks(scale, inverse_ref, tgt_ref, a_ref, gw_ref[...], gc_ref[...], bd_ref, bp_ref, out_ref)


def add_kernel(a_ref, b_ref, out_ref):
    out_ref[...] = (a_ref[...] + b_ref[...]).astype(out_ref.dtype)


def sums_kernel(src_parts_ref, tgt_parts_ref, src_feats, src_factor, tgt_feats, tgt_factor):
    rank, width = src_factor.shape
    src_feats[...], src_factor[...] = unpack(jnp.sum(src_parts_ref[...].astype(F32), 0), rank, width)
    total = jnp.sum(tgt_parts_ref[...].astype(F32), 0)
    tgt_feats[...] = total[:-rank]
    tgt_factor[...] = total[-rank:]


def call(kernel, specs, outs, scratch=(), flops=0):
    single = not isinstance(outs, tuple)
    return pl.pallas_call(
        kernel,
        out_shape=outs,
        in_specs=specs,
        out_specs=VMEM if single else tuple(VMEM for _ in outs),
        scratch_shapes=scratch,
        compiler_params=pltpu.CompilerParams(vmem_limit_bytes=40 << 20),
        cost_estimate=pl.CostEstimate(flops=flops, transcendentals=0, bytes_accessed=1 << 20),
    )


def shape(*dims, dtype=F32):
    return jax.ShapeDtypeStruct(dims, dtype)


def exchange(blocks, axes):
    return lax.all_to_all(blocks, axes, 0, 0, tiled=True)


def swap(blocks):
    return lax.ppermute(blocks, CORE, [(0, 1), (1, 0)])


def local(src_feats, src_factor, tgt_feats, tgt_factor, rank_weight):
    features, src_width = src_feats.shape
    rank = src_factor.shape[0]
    rows = features + rank
    tgt_width = tgt_feats.shape[1]
    ring = lax.axis_size(RING)
    plane = lax.axis_size(PLANE)
    scale = 1.0 / (tgt_width * ring * plane * lax.axis_size(CORE))
    sources = ring * src_width
    targets = 2 * plane * tgt_width

    tgt_copies, src_copies, inverse_g = call(
        copies_kernel,
        (HBM,) * 5,
        (
            shape(plane, rows, tgt_width, dtype=BF16),
            shape(ring, features, LANES, dtype=BF16),
            shape(rank, tgt_width),
        ),
        (
            pltpu.SMEM((rank,), F32),
            pltpu.VMEM((features, tgt_width), BF16),
            pltpu.VMEM((rank, tgt_width), BF16),
            pltpu.VMEM((features, src_width), BF16),
            pltpu.VMEM((rank, src_width), BF16),
            pltpu.SemaphoreType.DMA((5,)),
        ),
    )(
        *(
            pltpu.with_memory_space_constraint(array, pltpu.HBM)
            for array in (rank_weight, tgt_feats, tgt_factor, src_feats, src_factor)
        )
    )
    tgt_own = exchange(tgt_copies, PLANE)
    tgt_own, src_copies = lax.optimization_barrier((tgt_own, src_copies))
    src_blocks = exchange(src_copies, RING)
    tgt_other = swap(tgt_own)

    half = plane * tgt_width
    a, gw, gc, own_bd, own_bp, other_bd, other_bp = call(
        lambda *refs: target_prepare_kernel(features, *refs),
        (VMEM, VMEM),
        (
            shape(targets, 64, dtype=BF16),
            shape(features + 8, targets, dtype=BF16),
            shape(rank, targets, dtype=BF16),
        )
        + (shape(64, half, dtype=BF16),) * 4,
        flops=1 << 22,
    )(tgt_own, tgt_other)

    flops = sources * targets * 2 * 256 * 4
    src_parts, src_all = call(
        lambda *refs: source_pair_kernel(scale, src_width, *refs),
        (VMEM,) * 4,
        (shape(ring, features, LANES, dtype=BF16), shape(rows, sources)),
        (
            pltpu.VMEM((64, sources), BF16),
            pltpu.VMEM((64, sources), BF16),
            pltpu.VMEM((rows, sources), F32),
        ),
        flops,
    )(src_blocks, a, gw, gc)
    src_sums = exchange(src_parts, RING)
    send, src_a, src_gw, src_gc = call(
        lambda *refs: first_target_kernel(scale, features, *refs),
        (VMEM,) * 5,
        (
            shape(plane, rows, tgt_width),
            shape(sources, 64, dtype=BF16),
            shape(features + 8, sources, dtype=BF16),
            shape(rank, sources, dtype=BF16),
        ),
        flops=flops // 2,
    )(inverse_g, src_all, tgt_other, other_bd, other_bp)
    received = swap(send)
    keep = call(
        lambda *refs: second_target_kernel(scale, *refs),
        (VMEM,) * 7,
        shape(plane, rows, tgt_width),
        flops=flops // 2,
    )(inverse_g, tgt_own, own_bd, own_bp, src_a, src_gw, src_gc)
    tgt_half = call(add_kernel, (VMEM, VMEM), shape(plane, rows, tgt_width, dtype=BF16))(keep, received)
    src_sums, tgt_half = lax.optimization_barrier((src_sums, tgt_half))
    tgt_sums = exchange(tgt_half, PLANE)

    return call(
        sums_kernel,
        (VMEM, VMEM),
        (
            shape(features, src_width),
            shape(rank, src_width),
            shape(features, tgt_width),
            shape(rank, tgt_width),
        ),
    )(src_sums, tgt_sums)


def solution(mesh):
    fine = Mesh(mesh.devices.reshape(8, 2, 2, 4, 4), ("zl", "core", "zh", "y", "x"))
    by_src = P(None, ("zl", "core", "zh", "y", "x"))
    by_tgt = P(None, ("zh", "y", "x", "zl", "core"))
    return jax.shard_map(
        local,
        mesh=fine,
        in_specs=(by_src, by_src, by_tgt, by_tgt, P()),
        out_specs=(by_src, by_src, by_tgt, by_tgt),
        check_vma=False,
    )
```

```python
import jax
import jax.numpy as jnp
from jax import lax
from jax.experimental import pallas as pl
from jax.experimental.pallas import tpu as pltpu
from jax.sharding import Mesh
from jax.sharding import PartitionSpec as P

RING = ("zh", "zl")
PLANE = ("y", "x")
CORE = "core"
BF16 = jnp.bfloat16
F32 = jnp.float32
VMEM = pl.BlockSpec(memory_space=pltpu.VMEM)
HBM = pl.BlockSpec(memory_space=pltpu.HBM)
LANES = 128


def dot(a, b):
    return jnp.dot(a, b, preferred_element_type=F32)


def inverse_column(rank_ref, width):
    rank = rank_ref.shape[0]
    rows = lax.broadcasted_iota(jnp.int32, (rank, width), 0)
    column = jnp.full((rank, width), rank_ref[0], F32)
    for k in range(1, rank):
        column = jnp.where(rows == k, rank_ref[k], column)
    return 1.0 / column


def pack(feats, factor):
    rows, width = feats.shape
    half = width // 2
    halves = jnp.concatenate([factor[:, :half], factor[:, half:]], 0)
    return jnp.concatenate([feats, halves, jnp.zeros((rows, LANES - width - half), F32)], 1)


def unpack(block, rank, width):
    half = width // 2
    halves = block[:, width : width + half]
    return block[:, :width], jnp.concatenate([halves[:rank], halves[rank:]], 1)


def copies_kernel(rank_hbm, tgt_hbm, tgt_factor_hbm, src_hbm, src_factor_hbm, tgt_out, src_out, inverse_ref, rank_ref, tgt_ref, tgt_factor_ref, src_ref, src_factor_ref, src_copies, sems, out_sem):
    pairs = [
        (rank_hbm, rank_ref),
        (tgt_hbm, tgt_ref),
        (tgt_factor_hbm, tgt_factor_ref),
        (src_hbm, src_ref),
        (src_factor_hbm, src_factor_ref),
    ]
    loads = [pltpu.make_async_copy(a, b, sems.at[k]) for k, (a, b) in enumerate(pairs)]
    for load in loads:
        load.start()
    for load in loads[3:]:
        load.wait()
    src_block = pack(src_ref[...].astype(F32), src_factor_ref[...].astype(F32)).astype(BF16)
    for member in range(src_copies.shape[0]):
        src_copies[member] = src_block
    store = pltpu.make_async_copy(src_copies, src_out, out_sem)
    store.start()
    for load in loads[:3]:
        load.wait()
    factor = tgt_factor_ref[...]
    inverse_g = inverse_column(rank_ref, factor.shape[1])
    inverse_ref[...] = inverse_g
    scaled = (factor.astype(F32) * inverse_g).astype(BF16)
    tgt_block = jnp.concatenate([tgt_ref[...], scaled], 0)
    for member in range(tgt_out.shape[0]):
        tgt_out[member] = tgt_block
    store.wait()


def three_parts(value):
    high = value.astype(BF16).astype(F32)
    rest = value - high
    mid = rest.astype(BF16).astype(F32)
    low = (rest - mid).astype(BF16).astype(F32)
    return [high, mid, low]


def squares(feats):
    return jnp.sum(jnp.square(feats), 0, keepdims=True)


def put_sublanes(at, x, q, a_ref, gw_ref, gc_ref):
    width = x.shape[1]
    ones = jnp.ones((1, width), F32)
    stack = jnp.concatenate(
        [-2.0 * x, q] + three_parts(squares(x)) + [ones] * 3 + [jnp.zeros((10, width), F32)], 0
    )
    a_ref[at, :] = stack.T.astype(BF16)
    gw_ref[:, at] = jnp.concatenate([x, ones, jnp.zeros((7, width), F32)], 0).astype(BF16)
    gc_ref[:, at] = q.astype(BF16)


def lane_operands(x, q):
    features, width = x.shape
    rank = q.shape[0]
    distance = jnp.concatenate(
        [x, jnp.zeros((rank, width), F32), jnp.ones((3, width), F32)]
        + three_parts(squares(x) + 1.0)
        + [jnp.zeros((10, width), F32)],
        0,
    )
    plan = jnp.concatenate([jnp.zeros((features, width), F32), q, jnp.zeros((16, width), F32)], 0)
    return distance.astype(BF16), plan.astype(BF16)


def pair_sums(a_ref, gw, gc, bd, bp, step):
    lanes = bd.shape[1]
    sum_w = jnp.zeros((gw.shape[0], lanes), F32)
    sum_c = jnp.zeros((gc.shape[0], lanes), F32)
    for u in range(0, a_ref.shape[0], step):
        a = a_ref[pl.ds(u, step), :]
        s = dot(a, bd)
        p = dot(a, bp)
        r = lax.rsqrt(s)
        sum_w += dot(gw[:, u : u + step], (p * r).astype(BF16))
        sum_c += dot(gc[:, u : u + step], (s * r).astype(BF16))
    return sum_w, sum_c


def feature_gradient(x, sum_w, scale):
    features = x.shape[0]
    return (x * sum_w[features : features + 1] - sum_w[:features]) * scale


def target_prepare_kernel(features, own_ref, other_ref, a_ref, gw_ref, gc_ref, own_bd, own_bp, other_bd, other_bp):
    count, _, width = own_ref.shape
    for half, (ref, bd_ref, bp_ref) in enumerate([(own_ref, own_bd, own_bp), (other_ref, other_bd, other_bp)]):
        for b in range(count):
            block = ref[b].astype(F32)
            put_sublanes(
                pl.ds((half * count + b) * width, width), block[:features], block[features:], a_ref, gw_ref, gc_ref
            )
            lanes = pl.ds(b * width, width)
            bd_ref[:, lanes], bp_ref[:, lanes] = lane_operands(block[:features], block[features:])


def source_pair_kernel(scale, width, src_ref, a_ref, gw_ref, gc_ref, out_hbm, all_ref, bd_ref, bp_ref, out_ref, sems):
    count, features, _ = src_ref.shape
    rank = gc_ref.shape[0]
    for b in range(count):
        lanes = slice(b * width, (b + 1) * width)
        all_ref[:features, lanes], all_ref[features:, lanes] = unpack(src_ref[b].astype(F32), rank, width)
    bd_ref[...], bp_ref[...] = lane_operands(all_ref[:features], all_ref[features:])
    gw = gw_ref[...]
    gc = gc_ref[...]
    total = all_ref.shape[1]
    step = total // 2
    group = count // 2
    stores = []
    for half in range(2):
        at = slice(half * step, (half + 1) * step)
        sum_w, sum_c = pair_sums(a_ref, gw, gc, bd_ref[:, at], bp_ref[:, at], 1024)
        feats = feature_gradient(all_ref[:features, at], sum_w, scale)
        factor = sum_c * scale
        for b in range(group):
            lanes = slice(b * width, (b + 1) * width)
            out_ref[half * group + b] = pack(feats[:, lanes], factor[:, lanes]).astype(out_ref.dtype)
        part = pl.ds(half * group, group)
        stores.append(pltpu.make_async_copy(out_ref.at[part], out_hbm.at[part], sems.at[half]))
        stores[-1].start()
    for store in stores:
        store.wait()


def target_chunks(scale, inverse_ref, from_ref, a_ref, gw, gc, bd_ref, bp_ref, to_ref):
    count, rows, width = from_ref.shape
    features = rows - gc.shape[0]
    factor_scale = inverse_ref[...] * scale
    group = 8
    step = group * width

    def advance(index, carry):
        at = pl.ds(pl.multiple_of(index * step, step), step)
        sum_w, sum_c = pair_sums(a_ref, gw, gc, bd_ref[:, at], bp_ref[:, at], a_ref.shape[0] // 2)
        for k in range(group):
            lanes = slice(k * width, (k + 1) * width)
            x = from_ref[index * group + k][:features].astype(F32)
            grad = feature_gradient(x, sum_w[:, lanes], scale)
            to_ref[index * group + k] = jnp.concatenate([grad, sum_c[:, lanes] * factor_scale], 0)
        return carry

    lax.fori_loop(0, count // group, advance, 0)


def first_target_kernel(scale, features, inverse_ref, src_ref, tgt_ref, bd_ref, bp_ref, out_ref, a_ref, gw_ref, gc_ref):
    put_sublanes(slice(None), src_ref[:features], src_ref[features:], a_ref, gw_ref, gc_ref)
    target_chunks(scale, inverse_ref, tgt_ref, a_ref, gw_ref[...], gc_ref[...], bd_ref, bp_ref, out_ref)


def second_target_kernel(scale, inverse_ref, tgt_ref, bd_ref, bp_ref, a_ref, gw_ref, gc_ref, out_ref):
    target_chunks(scale, inverse_ref, tgt_ref, a_ref, gw_ref[...], gc_ref[...], bd_ref, bp_ref, out_ref)


def add_kernel(a_ref, b_ref, out_ref):
    out_ref[...] = (a_ref[...] + b_ref[...]).astype(out_ref.dtype)


def sums_kernel(src_parts_ref, tgt_parts_ref, src_feats, src_factor, tgt_feats, tgt_factor):
    rank, width = src_factor.shape
    src_feats[...], src_factor[...] = unpack(jnp.sum(src_parts_ref[...].astype(F32), 0), rank, width)
    total = jnp.sum(tgt_parts_ref[...].astype(F32), 0)
    tgt_feats[...] = total[:-rank]
    tgt_factor[...] = total[-rank:]


def call(kernel, specs, outs, scratch=(), flops=0, out_specs=None):
    single = not isinstance(outs, tuple)
    return pl.pallas_call(
        kernel,
        out_shape=outs,
        in_specs=specs,
        out_specs=out_specs or (VMEM if single else tuple(VMEM for _ in outs)),
        scratch_shapes=scratch,
        compiler_params=pltpu.CompilerParams(vmem_limit_bytes=40 << 20),
        cost_estimate=pl.CostEstimate(flops=flops, transcendentals=0, bytes_accessed=1 << 20),
    )


def shape(*dims, dtype=F32):
    return jax.ShapeDtypeStruct(dims, dtype)


def exchange(blocks, axes):
    return lax.all_to_all(blocks, axes, 0, 0, tiled=True)


def swap(blocks):
    return lax.ppermute(blocks, CORE, [(0, 1), (1, 0)])


def local(src_feats, src_factor, tgt_feats, tgt_factor, rank_weight):
    features, src_width = src_feats.shape
    rank = src_factor.shape[0]
    rows = features + rank
    tgt_width = tgt_feats.shape[1]
    ring = lax.axis_size(RING)
    plane = lax.axis_size(PLANE)
    scale = 1.0 / (tgt_width * ring * plane * lax.axis_size(CORE))
    sources = ring * src_width
    targets = 2 * plane * tgt_width

    tgt_copies, src_copies, inverse_g = call(
        copies_kernel,
        (HBM,) * 5,
        (
            shape(plane, rows, tgt_width, dtype=BF16),
            shape(ring, features, LANES, dtype=BF16),
            shape(rank, tgt_width),
        ),
        (
            pltpu.SMEM((rank,), F32),
            pltpu.VMEM((features, tgt_width), BF16),
            pltpu.VMEM((rank, tgt_width), BF16),
            pltpu.VMEM((features, src_width), BF16),
            pltpu.VMEM((rank, src_width), BF16),
            pltpu.VMEM((ring, features, LANES), BF16),
            pltpu.SemaphoreType.DMA((5,)),
            pltpu.SemaphoreType.DMA,
        ),
        out_specs=(VMEM, HBM, VMEM),
    )(
        *(
            pltpu.with_memory_space_constraint(array, pltpu.HBM)
            for array in (rank_weight, tgt_feats, tgt_factor, src_feats, src_factor)
        )
    )
    tgt_own = exchange(tgt_copies, PLANE)
    tgt_own, src_copies = lax.optimization_barrier((tgt_own, src_copies))
    src_blocks = exchange(src_copies, RING)
    tgt_other = swap(tgt_own)

    half = plane * tgt_width
    a, gw, gc, own_bd, own_bp, other_bd, other_bp = call(
        lambda *refs: target_prepare_kernel(features, *refs),
        (VMEM, VMEM),
        (
            shape(targets, 64, dtype=BF16),
            shape(features + 8, targets, dtype=BF16),
            shape(rank, targets, dtype=BF16),
        )
        + (shape(64, half, dtype=BF16),) * 4,
        flops=1 << 22,
    )(tgt_own, tgt_other)

    flops = sources * targets * 2 * 256 * 4
    src_parts, src_all = call(
        lambda *refs: source_pair_kernel(scale, src_width, *refs),
        (VMEM,) * 4,
        (shape(ring, features, LANES, dtype=BF16), shape(rows, sources)),
        (
            pltpu.VMEM((64, sources), BF16),
            pltpu.VMEM((64, sources), BF16),
            pltpu.VMEM((ring, features, LANES), BF16),
            pltpu.SemaphoreType.DMA((2,)),
        ),
        flops,
        (HBM, VMEM),
    )(src_blocks, a, gw, gc)
    src_sums = exchange(src_parts, RING)
    send, src_a, src_gw, src_gc = call(
        lambda *refs: first_target_kernel(scale, features, *refs),
        (VMEM,) * 5,
        (
            shape(plane, rows, tgt_width),
            shape(sources, 64, dtype=BF16),
            shape(features + 8, sources, dtype=BF16),
            shape(rank, sources, dtype=BF16),
        ),
        flops=flops // 2,
    )(inverse_g, src_all, tgt_other, other_bd, other_bp)
    received = swap(send)
    keep = call(
        lambda *refs: second_target_kernel(scale, *refs),
        (VMEM,) * 7,
        shape(plane, rows, tgt_width),
        flops=flops // 2,
    )(inverse_g, tgt_own, own_bd, own_bp, src_a, src_gw, src_gc)
    tgt_half = call(add_kernel, (VMEM, VMEM), shape(plane, rows, tgt_width, dtype=BF16))(keep, received)
    src_sums, tgt_half = lax.optimization_barrier((src_sums, tgt_half))
    tgt_sums = exchange(tgt_half, PLANE)

    return call(
        sums_kernel,
        (VMEM, VMEM),
        (
            shape(features, src_width),
            shape(rank, src_width),
            shape(features, tgt_width),
            shape(rank, tgt_width),
        ),
    )(src_sums, tgt_sums)


def solution(mesh):
    fine = Mesh(mesh.devices.reshape(8, 2, 2, 4, 4), ("zl", "core", "zh", "y", "x"))
    by_src = P(None, ("zl", "core", "zh", "y", "x"))
    by_tgt = P(None, ("zh", "y", "x", "zl", "core"))
    return jax.shard_map(
        local,
        mesh=fine,
        in_specs=(by_src, by_src, by_tgt, by_tgt, P()),
        out_specs=(by_src, by_src, by_tgt, by_tgt),
        check_vma=False,
    )
```

```python
import jax
import jax.numpy as jnp
from jax import lax
from jax.experimental import pallas as pl
from jax.experimental.pallas import tpu as pltpu
from jax.sharding import Mesh
from jax.sharding import PartitionSpec as P

RING = ("zl", "zh")
PLANE = ("y", "x")
CORE = "core"
BF16 = jnp.bfloat16
F32 = jnp.float32
VMEM = pl.BlockSpec(memory_space=pltpu.VMEM)
HBM = pl.BlockSpec(memory_space=pltpu.HBM)
LANES = 128


def dot(a, b):
    return jnp.dot(a, b, preferred_element_type=F32)


def inverse_column(rank_ref, width):
    rank = rank_ref.shape[0]
    rows = lax.broadcasted_iota(jnp.int32, (rank, width), 0)
    column = jnp.full((rank, width), rank_ref[0], F32)
    for k in range(1, rank):
        column = jnp.where(rows == k, rank_ref[k], column)
    return 1.0 / column


def pack(feats, factor):
    rows, width = feats.shape
    half = width // 2
    halves = jnp.concatenate([factor[:, :half], factor[:, half:]], 0)
    return jnp.concatenate([feats, halves, jnp.zeros((rows, LANES - width - half), F32)], 1)


def unpack(block, rank, width):
    half = width // 2
    halves = block[:, width : width + half]
    return block[:, :width], jnp.concatenate([halves[:rank], halves[rank:]], 1)


def copies_kernel(rank_hbm, tgt_hbm, tgt_factor_hbm, src_hbm, src_factor_hbm, tgt_out, src_out, inverse_ref, rank_ref, tgt_ref, tgt_factor_ref, src_ref, src_factor_ref, sems):
    pairs = [
        (rank_hbm, rank_ref),
        (tgt_hbm, tgt_ref),
        (tgt_factor_hbm, tgt_factor_ref),
        (src_hbm, src_ref),
        (src_factor_hbm, src_factor_ref),
    ]
    loads = [pltpu.make_async_copy(a, b, sems.at[k]) for k, (a, b) in enumerate(pairs)]
    for load in loads:
        load.start()
    for load in loads:
        load.wait()
    factor = tgt_factor_ref[...]
    inverse_g = inverse_column(rank_ref, factor.shape[1])
    inverse_ref[...] = inverse_g
    scaled = (factor.astype(F32) * inverse_g).astype(BF16)
    tgt_block = jnp.concatenate([tgt_ref[...], scaled], 0)
    for member in range(tgt_out.shape[0]):
        tgt_out[member] = tgt_block
    src_block = pack(src_ref[...].astype(F32), src_factor_ref[...].astype(F32)).astype(BF16)
    for member in range(src_out.shape[0]):
        src_out[member] = src_block


def three_parts(value):
    high = value.astype(BF16).astype(F32)
    rest = value - high
    mid = rest.astype(BF16).astype(F32)
    low = (rest - mid).astype(BF16).astype(F32)
    return [high, mid, low]


def squares(feats):
    return jnp.sum(jnp.square(feats), 0, keepdims=True)


def put_sublanes(at, x, q, a_ref, gw_ref, gc_ref):
    width = x.shape[1]
    ones = jnp.ones((1, width), F32)
    stack = jnp.concatenate(
        [-2.0 * x, q] + three_parts(squares(x)) + [ones] * 3 + [jnp.zeros((10, width), F32)], 0
    )
    a_ref[at, :] = stack.T.astype(BF16)
    gw_ref[:, at] = jnp.concatenate([x, ones, jnp.zeros((7, width), F32)], 0).astype(BF16)
    gc_ref[:, at] = q.astype(BF16)


def lane_operands(x, q):
    features, width = x.shape
    rank = q.shape[0]
    distance = jnp.concatenate(
        [x, jnp.zeros((rank, width), F32), jnp.ones((3, width), F32)]
        + three_parts(squares(x) + 1.0)
        + [jnp.zeros((10, width), F32)],
        0,
    )
    plan = jnp.concatenate([jnp.zeros((features, width), F32), q, jnp.zeros((16, width), F32)], 0)
    return distance.astype(BF16), plan.astype(BF16)


def pair_sums(a_ref, gw, gc, bd, bp, step):
    lanes = bd.shape[1]
    sum_w = jnp.zeros((gw.shape[0], lanes), F32)
    sum_c = jnp.zeros((gc.shape[0], lanes), F32)
    for u in range(0, a_ref.shape[0], step):
        a = a_ref[pl.ds(u, step), :]
        s = dot(a, bd)
        p = dot(a, bp)
        r = lax.rsqrt(s)
        sum_w += dot(gw[:, u : u + step], (p * r).astype(BF16))
        sum_c += dot(gc[:, u : u + step], (s * r).astype(BF16))
    return sum_w, sum_c


def feature_gradient(x, sum_w, scale):
    features = x.shape[0]
    return (x * sum_w[features : features + 1] - sum_w[:features]) * scale


def target_prepare_kernel(features, own_ref, other_ref, a_ref, gw_ref, gc_ref, own_bd, own_bp, other_bd, other_bp):
    count, _, width = own_ref.shape
    for half, (ref, bd_ref, bp_ref) in enumerate([(own_ref, own_bd, own_bp), (other_ref, other_bd, other_bp)]):
        for b in range(count):
            block = ref[b].astype(F32)
            put_sublanes(
                pl.ds((half * count + b) * width, width), block[:features], block[features:], a_ref, gw_ref, gc_ref
            )
            lanes = pl.ds(b * width, width)
            bd_ref[:, lanes], bp_ref[:, lanes] = lane_operands(block[:features], block[features:])


def source_pair_kernel(scale, width, src_ref, a_ref, gw_ref, gc_ref, out_ref, all_ref, bd_ref, bp_ref, sum_ref):
    count, features, _ = src_ref.shape
    rank = gc_ref.shape[0]
    for b in range(count):
        lanes = slice(b * width, (b + 1) * width)
        all_ref[:features, lanes], all_ref[features:, lanes] = unpack(src_ref[b].astype(F32), rank, width)
    bd_ref[...], bp_ref[...] = lane_operands(all_ref[:features], all_ref[features:])
    gw = gw_ref[...]
    gc = gc_ref[...]
    total = all_ref.shape[1]
    step = total // 2
    for start in range(0, total, step):
        at = slice(start, start + step)
        sum_w, sum_c = pair_sums(a_ref, gw, gc, bd_ref[:, at], bp_ref[:, at], 1024)
        sum_ref[:features, at] = feature_gradient(all_ref[:features, at], sum_w, scale)
        sum_ref[features:, at] = sum_c * scale
    for b in range(count):
        block = sum_ref[:, b * width : (b + 1) * width]
        out_ref[b] = pack(block[:features], block[features:]).astype(out_ref.dtype)


def target_chunks(scale, inverse_ref, from_ref, a_ref, gw, gc, bd_ref, bp_ref, to_ref):
    count, rows, width = from_ref.shape
    features = rows - gc.shape[0]
    factor_scale = inverse_ref[...] * scale
    group = 8
    step = group * width

    def advance(index, carry):
        at = pl.ds(pl.multiple_of(index * step, step), step)
        sum_w, sum_c = pair_sums(a_ref, gw, gc, bd_ref[:, at], bp_ref[:, at], a_ref.shape[0] // 2)
        for k in range(group):
            lanes = slice(k * width, (k + 1) * width)
            x = from_ref[index * group + k][:features].astype(F32)
            grad = feature_gradient(x, sum_w[:, lanes], scale)
            to_ref[index * group + k] = jnp.concatenate([grad, sum_c[:, lanes] * factor_scale], 0)
        return carry

    lax.fori_loop(0, count // group, advance, 0)


def first_target_kernel(scale, features, inverse_ref, src_ref, tgt_ref, bd_ref, bp_ref, out_ref, a_ref, gw_ref, gc_ref):
    put_sublanes(slice(None), src_ref[:features], src_ref[features:], a_ref, gw_ref, gc_ref)
    target_chunks(scale, inverse_ref, tgt_ref, a_ref, gw_ref[...], gc_ref[...], bd_ref, bp_ref, out_ref)


def second_target_kernel(scale, inverse_ref, tgt_ref, bd_ref, bp_ref, a_ref, gw_ref, gc_ref, out_ref):
    target_chunks(scale, inverse_ref, tgt_ref, a_ref, gw_ref[...], gc_ref[...], bd_ref, bp_ref, out_ref)


def add_kernel(a_ref, b_ref, out_ref):
    out_ref[...] = (a_ref[...] + b_ref[...]).astype(out_ref.dtype)


def sums_kernel(src_parts_ref, tgt_parts_ref, src_feats, src_factor, tgt_feats, tgt_factor):
    rank, width = src_factor.shape
    src_feats[...], src_factor[...] = unpack(jnp.sum(src_parts_ref[...].astype(F32), 0), rank, width)
    total = jnp.sum(tgt_parts_ref[...].astype(F32), 0)
    tgt_feats[...] = total[:-rank]
    tgt_factor[...] = total[-rank:]


def call(kernel, specs, outs, scratch=(), flops=0):
    single = not isinstance(outs, tuple)
    return pl.pallas_call(
        kernel,
        out_shape=outs,
        in_specs=specs,
        out_specs=VMEM if single else tuple(VMEM for _ in outs),
        scratch_shapes=scratch,
        compiler_params=pltpu.CompilerParams(vmem_limit_bytes=40 << 20),
        cost_estimate=pl.CostEstimate(flops=flops, transcendentals=0, bytes_accessed=1 << 20),
    )


def shape(*dims, dtype=F32):
    return jax.ShapeDtypeStruct(dims, dtype)


def exchange(blocks, axes):
    return lax.all_to_all(blocks, axes, 0, 0, tiled=True)


def swap(blocks):
    return lax.ppermute(blocks, CORE, [(0, 1), (1, 0)])


def local(src_feats, src_factor, tgt_feats, tgt_factor, rank_weight):
    features, src_width = src_feats.shape
    rank = src_factor.shape[0]
    rows = features + rank
    tgt_width = tgt_feats.shape[1]
    ring = lax.axis_size(RING)
    plane = lax.axis_size(PLANE)
    scale = 1.0 / (tgt_width * ring * plane * lax.axis_size(CORE))
    sources = ring * src_width
    targets = 2 * plane * tgt_width

    tgt_copies, src_copies, inverse_g = call(
        copies_kernel,
        (HBM,) * 5,
        (
            shape(plane, rows, tgt_width, dtype=BF16),
            shape(ring, features, LANES, dtype=BF16),
            shape(rank, tgt_width),
        ),
        (
            pltpu.SMEM((rank,), F32),
            pltpu.VMEM((features, tgt_width), BF16),
            pltpu.VMEM((rank, tgt_width), BF16),
            pltpu.VMEM((features, src_width), BF16),
            pltpu.VMEM((rank, src_width), BF16),
            pltpu.SemaphoreType.DMA((5,)),
        ),
    )(
        *(
            pltpu.with_memory_space_constraint(array, pltpu.HBM)
            for array in (rank_weight, tgt_feats, tgt_factor, src_feats, src_factor)
        )
    )
    tgt_own = exchange(tgt_copies, PLANE)
    tgt_own, src_copies = lax.optimization_barrier((tgt_own, src_copies))
    src_blocks = exchange(src_copies, RING)
    tgt_other = swap(tgt_own)

    half = plane * tgt_width
    a, gw, gc, own_bd, own_bp, other_bd, other_bp = call(
        lambda *refs: target_prepare_kernel(features, *refs),
        (VMEM, VMEM),
        (
            shape(targets, 64, dtype=BF16),
            shape(features + 8, targets, dtype=BF16),
            shape(rank, targets, dtype=BF16),
        )
        + (shape(64, half, dtype=BF16),) * 4,
        flops=1 << 22,
    )(tgt_own, tgt_other)

    flops = sources * targets * 2 * 256 * 4
    src_parts, src_all = call(
        lambda *refs: source_pair_kernel(scale, src_width, *refs),
        (VMEM,) * 4,
        (shape(ring, features, LANES, dtype=BF16), shape(rows, sources)),
        (
            pltpu.VMEM((64, sources), BF16),
            pltpu.VMEM((64, sources), BF16),
            pltpu.VMEM((rows, sources), F32),
        ),
        flops,
    )(src_blocks, a, gw, gc)
    src_sums = exchange(src_parts, RING)
    send, src_a, src_gw, src_gc = call(
        lambda *refs: first_target_kernel(scale, features, *refs),
        (VMEM,) * 5,
        (
            shape(plane, rows, tgt_width),
            shape(sources, 64, dtype=BF16),
            shape(features + 8, sources, dtype=BF16),
            shape(rank, sources, dtype=BF16),
        ),
        flops=flops // 2,
    )(inverse_g, src_all, tgt_other, other_bd, other_bp)
    received = swap(send)
    keep = call(
        lambda *refs: second_target_kernel(scale, *refs),
        (VMEM,) * 7,
        shape(plane, rows, tgt_width),
        flops=flops // 2,
    )(inverse_g, tgt_own, own_bd, own_bp, src_a, src_gw, src_gc)
    tgt_half = call(add_kernel, (VMEM, VMEM), shape(plane, rows, tgt_width, dtype=BF16))(keep, received)
    src_sums, tgt_half = lax.optimization_barrier((src_sums, tgt_half))
    tgt_sums = exchange(tgt_half, PLANE)

    return call(
        sums_kernel,
        (VMEM, VMEM),
        (
            shape(features, src_width),
            shape(rank, src_width),
            shape(features, tgt_width),
            shape(rank, tgt_width),
        ),
    )(src_sums, tgt_sums)


def solution(mesh):
    fine = Mesh(mesh.devices.reshape(8, 2, 2, 4, 4), ("zl", "core", "zh", "y", "x"))
    by_src = P(None, ("zl", "core", "zh", "y", "x"))
    by_tgt = P(None, ("zh", "y", "x", "zl", "core"))
    return jax.shard_map(
        local,
        mesh=fine,
        in_specs=(by_src, by_src, by_tgt, by_tgt, P()),
        out_specs=(by_src, by_src, by_tgt, by_tgt),
        check_vma=False,
    )
```
